32 devices in a mesh: groups: 2 (over y), seq: 4 (over z), dp: 4 (over x, core).
Axes of the slice: x: 2, y: 2, z: 4, core: 2. Of those that a mesh axis runs over, the one named last changes fastest.
Arguments:
- acceptance_gate: bfloat16 [8, 512, 1280], P(('groups', 'dp'), 'seq'), parts along dimension 0, may hold values from -6 to 6
- logarithmic_fade_factor: bfloat16 [8, 512, 1280], P(('groups', 'dp'), 'seq'), parts along dimension 0, may hold values from -12 to 0
- probe_matrix: bfloat16 [8, 512, 1280], P(('groups', 'dp'), 'seq'), parts along dimension 0, may hold values from -0.75 to 0.75
- payload_matrix: bfloat16 [8, 512, 1280], P(('groups', 'dp'), 'seq'), parts along dimension 0, may hold values from -6 to 6
- erasure_vector: bfloat16 [8, 512, 1280], P(('groups', 'dp'), 'seq'), parts along dimension 0, may hold values from -6 to 6
- inplace_update_step: bfloat16 [8, 512, 1280], P(('groups', 'dp'), 'seq'), parts along dimension 0, may hold values from 0.0079956055 to 0.019897461
- extra_probe_factor: float32 [1280], replicated, may hold values from -3 to 3
- group_scaling_factor: float32 [1280], replicated, may hold values from 0.5 to 1.5
Outputs:
- blended_signal: bfloat16 [8, 512, 1280], P(('groups', 'dp'), 'seq'), parts along dimension 0
- final_state: float32 [8, 1280, 64], P(('groups', 'dp'), 'seq'), parts along dimension 0
The draws below stay inside these ranges and needn't reach their ends.
There are 2 independent parts, one for each index of `groups`. The reference program is written for one: setup_inputs(seed, part) draws one part's arguments, and reference() takes and returns one part's arrays. A program takes and returns all parts, laid end to end along the dimension named above; an argument that names none is the same for every part. Nothing has to cross between parts.
All inputs are finite; a program needn't handle non-finite values.
Results may differ from the reference program's by a relative error of at most 0.001.
Values sent between devices are 32-bit elements; how exact they have to be, the bound alone decides.
No kernel may reach another device: no remote copies, remote signals or barrier semaphores. Data moves between devices by JAX's collectives and lax.ppermute only.
A program may use at most 64 MiB of HBM per device.

```python
import jax
import jax.numpy as jnp
from jax import lax

GROUP_DIMENSION = 64
HEADS = 20
BLOCK = 64
TOKEN_COUNT = 512
BATCH_COUNT = 4
MODEL_DIMENSION = 1280


def draw_logarithmic_fade_factor(key, part):
    key_rows = jax.random.split(key, 6)
    fast_share = 0.5
    fast_head = jax.random.uniform(key_rows[0], (BATCH_COUNT, 1, HEADS, 1)) < fast_share
    span = jax.random.uniform(key_rows[1], (BATCH_COUNT, 1, HEADS, 1), minval=30.0, maxval=50.0)
    slow_rate = 2.302585 / TOKEN_COUNT * jax.random.uniform(key_rows[2], (BATCH_COUNT, 1, HEADS, 1), minval=0.1, maxval=0.4)
    base_rate = jnp.where(fast_head, 1.0 / span, slow_rate)
    rough = jnp.exp(jax.random.uniform(key_rows[3], (BATCH_COUNT, TOKEN_COUNT, HEADS, GROUP_DIMENSION), minval=-0.7, maxval=0.7))
    rate = base_rate * rough
    split_point = jax.random.randint(key_rows[4], (BATCH_COUNT, 1, 2), 0, TOKEN_COUNT)
    token_positions = jnp.arange(TOKEN_COUNT, dtype=jnp.int32).reshape(1, TOKEN_COUNT, 1)
    splitting_now = jnp.any(token_positions == split_point, axis=-1)[:, :, None, None]
    retained = jax.random.uniform(key_rows[5], (BATCH_COUNT, TOKEN_COUNT, HEADS, GROUP_DIMENSION), minval=0.5, maxval=0.8)
    rate = jnp.where(jnp.logical_and(splitting_now, jnp.logical_not(fast_head)), -jnp.log(retained), rate)
    return jnp.log(rate).reshape(BATCH_COUNT, TOKEN_COUNT, HEADS * GROUP_DIMENSION).astype(jnp.bfloat16)


def draw_erasure_vector(key, part):
    key_rows = jax.random.split(key, 2)
    block_total = TOKEN_COUNT // BLOCK
    common = jnp.clip(jax.random.normal(key_rows[0], (BATCH_COUNT, block_total, 1, HEADS, GROUP_DIMENSION)), -3.0, 3.0)
    jitter = 0.5 * jnp.clip(jax.random.normal(key_rows[1], (BATCH_COUNT, block_total, BLOCK, HEADS, GROUP_DIMENSION)), -3.0, 3.0)
    values = jnp.clip(common + jitter, -6.0, 6.0)
    return values.reshape(BATCH_COUNT, TOKEN_COUNT, HEADS * GROUP_DIMENSION).astype(jnp.bfloat16)


def level_of(stream_key, dims, pieces, low, high):
    gain = 1.0
    for axis_at, shards_of in pieces:
        heights = jax.random.uniform(jax.random.fold_in(jax.random.fold_in(stream_key, 6), axis_at), (shards_of,), jnp.float32, low / len(pieces), high / len(pieces))
        gain = gain * jnp.repeat(jnp.exp(heights), dims[axis_at] // shards_of).reshape((-1,) + (1,) * (len(dims) - 1 - axis_at))
    return gain


def centred(rng, shape, scale, most, cuts=(), kind=jnp.bfloat16):
    gain = level_of(rng, shape, cuts, -0.22, 0.18) if cuts else 1.0
    values = jax.random.normal(rng, shape, jnp.float32) * scale * gain
    return jnp.minimum(jnp.maximum(values, -most), most).astype(kind)


def setup_inputs(seed: int = 0, part: int = 0) -> dict:
    splits = jax.random.split(jax.random.key(seed), 9)
    part_keys = jax.random.split(jax.random.fold_in(splits[8], part), 9)
    acceptance_gate = centred(part_keys[0], (BATCH_COUNT, TOKEN_COUNT, MODEL_DIMENSION), 1.0, 6.0, ((0, 4), (1, 4)))
    logarithmic_fade_factor = draw_logarithmic_fade_factor(jax.random.fold_in(jax.random.fold_in(splits[8], part), 71), part)
    probe_matrix = centred(part_keys[2], (BATCH_COUNT, TOKEN_COUNT, MODEL_DIMENSION), 0.125, 0.75, ((0, 4), (1, 4)))
    payload_matrix = centred(part_keys[3], (BATCH_COUNT, TOKEN_COUNT, MODEL_DIMENSION), 1.0, 6.0, ((0, 4), (1, 4)))
    erasure_vector = draw_erasure_vector(jax.random.fold_in(jax.random.fold_in(splits[8], part), 71), part)
    inplace_update_step = jnp.clip(0.0079956055 + 0.0119018555 * jax.random.uniform(part_keys[5], (BATCH_COUNT, TOKEN_COUNT, MODEL_DIMENSION), jnp.float32) ** level_of(part_keys[5], (BATCH_COUNT, TOKEN_COUNT, MODEL_DIMENSION), ((0, 4), (1, 4)), -0.2, 0.2), 0.0079956055, 0.019897461).astype(jnp.bfloat16)
    extra_probe_factor = centred(splits[6], (MODEL_DIMENSION,), 0.5, 3.0, (), jnp.float32)
    group_scaling_factor = jnp.clip(1.0 + 0.1 * jax.random.normal(splits[7], (MODEL_DIMENSION,), jnp.float32), 0.5, 1.5)
    return dict(acceptance_gate=acceptance_gate, logarithmic_fade_factor=logarithmic_fade_factor, probe_matrix=probe_matrix, payload_matrix=payload_matrix, erasure_vector=erasure_vector, inplace_update_step=inplace_update_step, extra_probe_factor=extra_probe_factor, group_scaling_factor=group_scaling_factor)


HIGHEST_PRECISION = lax.Precision.HIGHEST
KEY_EPS = 1e-05
NORM_EPS = 0.00064

def reference(acceptance_gate, logarithmic_fade_factor, probe_matrix, payload_matrix, erasure_vector, inplace_update_step, extra_probe_factor, group_scaling_factor):
    series_entries, series_extent, feature_total = acceptance_gate.shape
    group_total = feature_total // GROUP_DIMENSION

    def grouped_entries(array):
        return array.astype(jnp.float32).reshape(series_entries, series_extent, group_total, GROUP_DIMENSION)
    removal = grouped_entries(erasure_vector)
    kappa = removal * lax.rsqrt(lax.optimization_barrier(jnp.mean(removal * removal, -1, keepdims=True)) + KEY_EPS) * GROUP_DIMENSION ** (-0.5)
    kappa_flat = kappa.reshape(series_entries, series_extent, feature_total)

    def time_major(array):
        return jnp.swapaxes(array, 0, 1)

    def split_heads(array):
        return array.astype(jnp.float32).reshape(series_entries, group_total, GROUP_DIMENSION)

    def advance(state_now, inputs):
        reader_t, decay_t, key_t, value_t, kappa_t, rate_t = inputs
        receptance_per_head = split_heads(reader_t)
        decay_h = jnp.exp(-jnp.exp(split_heads(decay_t)))
        key_per_head = split_heads(key_t)
        value_per_head = split_heads(value_t)
        kappa_h = split_heads(kappa_t)
        rate_h = split_heads(rate_t)
        pulled = jnp.einsum('bhvk,bhk->bhv', state_now, -kappa_h, precision=HIGHEST_PRECISION)
        state_now = state_now * decay_h[:, :, None, :] + pulled[..., None] * (kappa_h * rate_h)[:, :, None, :] + value_per_head[..., None] * key_per_head[:, :, None, :]
        result = jnp.einsum('bhvk,bhk->bhv', state_now, receptance_per_head, precision=HIGHEST_PRECISION)
        return (state_now, result)
    initial = jnp.zeros((series_entries, group_total, GROUP_DIMENSION, GROUP_DIMENSION), jnp.float32)
    closing, outputs = lax.scan(advance, initial, (time_major(acceptance_gate), time_major(logarithmic_fade_factor), time_major(probe_matrix), time_major(payload_matrix), time_major(kappa_flat), time_major(inplace_update_step)))
    outputs = jnp.swapaxes(outputs, 0, 1)
    average = lax.optimization_barrier(jnp.mean(outputs, -1, keepdims=True))
    centered = outputs - average
    spread = lax.optimization_barrier(jnp.mean(centered * centered, -1, keepdims=True))
    standardized_result = centered * lax.rsqrt(spread + NORM_EPS) * group_scaling_factor.reshape(group_total, GROUP_DIMENSION)
    extra_result = lax.optimization_barrier(jnp.sum(grouped_entries(acceptance_gate) * grouped_entries(probe_matrix) * extra_probe_factor.reshape(group_total, GROUP_DIMENSION), -1, keepdims=True)) * grouped_entries(payload_matrix)
    blended_signal = (standardized_result + extra_result).reshape(series_entries, series_extent, feature_total).astype(jnp.bfloat16)
    final_state = closing.reshape(series_entries, feature_total, GROUP_DIMENSION)
    return (blended_signal, final_state)
```

```python
import functools

import jax
import jax.numpy as jnp
from jax import lax
from jax.experimental import pallas as pl
from jax.experimental.pallas import tpu as pltpu
from jax.sharding import PartitionSpec as P

GROUP_DIMENSION = 64
PAIR = 2 * GROUP_DIMENSION
KEY_EPS = 1e-05
NORM_EPS = 0.00064
STEP_PAIRS = 2

F32 = jnp.float32
BF16 = jnp.bfloat16


def mm(left, right):
    return jnp.dot(left, right, preferred_element_type=F32)


def split(x):
    high = x.astype(BF16)
    return high, (x - high.astype(F32)).astype(BF16)


def side(*parts):
    return jnp.concatenate(parts, axis=1)


def stack(*parts):
    return jnp.concatenate(parts, axis=0)


def mm3(left, right):
    lh, ll = left
    rh, rl = right
    return mm(side(lh, ll), stack(rh, rh)) + mm(lh, rl)


def iota(shape, axis):
    return lax.broadcasted_iota(jnp.int32, shape, axis)


def group_ones():
    same = (iota((PAIR, PAIR), 0) // GROUP_DIMENSION) == (
        iota((PAIR, PAIR), 1) // GROUP_DIMENSION
    )
    ones = same.astype(F32).astype(BF16)
    return stack(ones, ones)


def group_sums(x, ones):
    parts = []
    for p in range(x.shape[1] // PAIR):
        high, low = split(x[:, p * PAIR : (p + 1) * PAIR])
        parts.append(mm(side(high, low), ones))
    return side(*parts)


def block_diagonal(x):
    top, bottom = x[:GROUP_DIMENSION], x[GROUP_DIMENSION:]
    none = jnp.zeros_like(top)
    return stack(side(top, none), side(none, bottom))


def scores(first, second, query, late):
    qh, ql = (block_diagonal(q) for q in query)
    out_first = mm3(first, (qh, ql))
    out_second = mm3(second, (qh * late, ql * late))
    return out_first, out_second


def local_kernel(
    owners,
    reader_ref,
    fade_ref,
    key_ref,
    value_ref,
    removal_ref,
    rate_ref,
    extra_ref,
    *rest,
):
    send_refs = rest[:owners]
    lift_high_ref, lift_low_ref, within_ref, bonus_ref, held, sems = rest[owners:]
    step = pl.program_id(0)
    me = lax.axis_index("seq")
    tokens = reader_ref.shape[0]
    half = tokens // 2
    width = reader_ref.shape[1]
    pairs = width // PAIR
    per_owner = held.shape[1]

    row = iota((tokens, tokens), 0)
    col = iota((tokens, tokens), 1)
    lower = (row >= col).astype(F32).astype(BF16)
    ones = group_ones()
    late_lane = iota((PAIR, 2 * tokens), 1) % tokens
    late = (late_lane >= half).astype(F32).astype(BF16)

    reader = reader_ref[...].astype(F32)
    key = key_ref[...].astype(F32)
    value = value_ref[...].astype(F32)
    removal = removal_ref[...].astype(F32)
    rate = rate_ref[...].astype(F32)
    log_step = -jnp.exp(fade_ref[...].astype(F32))

    high, low = split(log_step)
    rest_low = (log_step - high.astype(F32) - low.astype(F32)).astype(BF16)
    cum = mm(side(lower, lower), stack(high, low)) + mm(lower, rest_low)
    middle = cum[half - 1 : half]
    end = cum[tokens - 1 : tokens]
    before = cum - log_step

    norm = group_sums(removal * removal, ones) * (1.0 / GROUP_DIMENSION)
    kappa = removal * lax.rsqrt(norm + KEY_EPS) * GROUP_DIMENSION ** (-0.5)

    inverse = jnp.exp(middle - cum)
    away = kappa * rate * inverse
    keys = key * inverse
    to_end = jnp.exp(end - middle)
    gamma_end = jnp.exp(end)
    toward_mid = -kappa * jnp.exp(before - middle)
    toward_abs = -kappa * jnp.exp(before)
    reader_mid = reader * jnp.exp(cum - middle)
    reader_abs = reader * jnp.exp(cum)

    bonus = group_sums(reader * key * extra_ref[...], ones)
    bonus_ref[...] = bonus * value

    lane = iota((GROUP_DIMENSION, PAIR), 1)
    sub = iota((GROUP_DIMENSION, PAIR), 0)

    for p in range(pairs):
        cut = slice(p * PAIR, (p + 1) * PAIR)
        away_p = split(away[:, cut])
        keys_p = split(keys[:, cut])
        first = tuple(stack(a[:half], k[:half]) for a, k in zip(away_p, keys_p))
        second = tuple(stack(a[half:], k[half:]) for a, k in zip(away_p, keys_p))
        t_mid = split(toward_mid[:, cut].T)
        r_mid = split(reader_mid[:, cut].T)
        t_abs = toward_abs[:, cut].T
        r_abs = reader_abs[:, cut].T
        value_t = value[:, cut].T.astype(BF16)
        mix_first, mix_second = scores(first, second, t_mid, late)
        read_first, read_second = scores(first, second, r_mid, late)
        away_end = split(away[:, cut] * to_end[:, cut])
        keys_end = split(keys[:, cut] * to_end[:, cut])

        for i in range(2):
            lanes = slice(i * tokens, (i + 1) * tokens)
            rows = slice(i * GROUP_DIMENSION, (i + 1) * GROUP_DIMENSION)

            def pick(a, b, top, keep):
                part = slice(0, half) if top else slice(half, 2 * half)
                return jnp.where(keep, stack(a[part, lanes], b[part, lanes]), 0.0)

            power = pick(mix_first, mix_second, True, row < col)
            mix_keys = pick(mix_first, mix_second, False, row < col)
            read_away = pick(read_first, read_second, True, row <= col)
            read_keys = pick(read_first, read_second, False, row <= col)
            value_h = value_t[rows]
            value_two = side(value_h, value_h)

            mk_high, mk_low = split(mix_keys)
            solved = stack(t_abs[rows], mm(value_two, stack(mk_high, mk_low)))
            ps = split(power)
            ws = split(solved)
            out = mm3(tuple(stack(w, q) for w, q in zip(ws, ps)), ps)
            solved = solved + out[:tokens]
            ps = split(out[tokens:])
            solved = solved + mm3(split(solved), ps)
            power = mm(ps[0], ps[0]).astype(BF16)
            reach = 4
            while reach < tokens:
                if reach * 2 < tokens:
                    out = mm(stack(solved.astype(BF16), power), power)
                    solved = solved + out[:tokens]
                    power = out[tokens:].astype(BF16)
                else:
                    solved = solved + mm(solved.astype(BF16), power)
                reach *= 2

            ws = split(solved)
            ended = mm3(ws, away_end)
            stay = jnp.where(
                lane == sub + i * GROUP_DIMENSION, gamma_end[:, cut], 0.0
            )
            state_map = ended[:GROUP_DIMENSION] + stay
            state_add = ended[GROUP_DIMENSION:] + mm(value_two, stack(*keys_end))
            if i == 0:
                state_add = pltpu.roll(state_add, GROUP_DIMENSION, 1)
            else:
                state_map = pltpu.roll(state_map, GROUP_DIMENSION, 1)
            both = jnp.where(lane < GROUP_DIMENSION, state_map, state_add)
            head = (step * pairs + p) * 2 + i
            slot = lax.rem(head // per_owner - me % owners + owners, owners)
            held[slot, lax.rem(head, per_owner)] = both

            read = mm3(ws, split(read_away))
            rk_high, rk_low = split(read_keys)
            within = read[GROUP_DIMENSION:] + mm(value_two, stack(rk_high, rk_low))
            lift_high, lift_low = split(r_abs[rows] + read[:GROUP_DIMENSION])
            at = slice(p * PAIR + i * GROUP_DIMENSION, p * PAIR + (i + 1) * GROUP_DIMENSION)
            lift_high_ref[at] = lift_high
            lift_low_ref[at] = lift_low
            within_ref[at] = within

    @pl.when(step == pl.num_programs(0) - 1)
    def _():
        copies = [
            pltpu.make_async_copy(held.at[k], send_refs[k], sems.at[k])
            for k in range(owners)
        ]
        for copy in copies:
            copy.start()
        for copy in copies:
            copy.wait()


def local_pass(owners, reader, fade, key, value, removal, rate, extra):
    tokens, features = reader.shape
    heads = features // GROUP_DIMENSION
    per_owner = heads // owners
    width = STEP_PAIRS * PAIR
    natural = pl.BlockSpec((tokens, width), lambda g: (0, g))
    turned = pl.BlockSpec((width, tokens), lambda g: (g, 0))
    vector = pl.BlockSpec((1, width), lambda g: (0, g))
    block = (per_owner, GROUP_DIMENSION, PAIR)
    out = pl.pallas_call(
        functools.partial(local_kernel, owners),
        grid=(features // width,),
        in_specs=[natural] * 6 + [vector],
        out_specs=[pl.BlockSpec(memory_space=pl.ANY)] * owners
        + [turned, turned, turned, natural],
        out_shape=[jax.ShapeDtypeStruct(block, F32)] * owners
        + [
            jax.ShapeDtypeStruct((features, tokens), BF16),
            jax.ShapeDtypeStruct((features, tokens), BF16),
            jax.ShapeDtypeStruct((features, tokens), F32),
            jax.ShapeDtypeStruct((tokens, features), F32),
        ],
        scratch_shapes=[
            pltpu.VMEM((owners,) + block, F32),
            pltpu.SemaphoreType.DMA((owners,)),
        ],
        name="local_pass",
    )(reader, fade, key, value, removal, rate, extra)
    return out[:owners], out[owners:]


def pack_rows(state):
    rows = state.shape[0] // 2
    return side(state[:rows], state[rows:])


def chain_kernel(owners, *refs):
    got_refs = refs[:owners]
    state_refs = refs[owners : 2 * owners]
    final_ref, ranges, states = refs[2 * owners :]
    me = lax.axis_index("seq")
    per_owner = got_refs[0].shape[0]
    for k in range(owners):
        ranges[lax.rem(me - k + owners, owners)] = got_refs[k][...]
    d = GROUP_DIMENSION
    current = []
    for q in range(per_owner):
        states[0, q] = jnp.zeros((d // 2, PAIR), F32)
        current.append(ranges[0, q][:, d:])
    for i in range(1, owners + 1):
        for q in range(per_owner):
            if i < owners:
                states[i, q] = pack_rows(current[q])
                both = ranges[i, q]
                maps = split(both)
                moved = mm3(split(current[q]), maps)[:, :d]
                current[q] = moved + both[:, d:]
            else:
                final_ref[q * d : (q + 1) * d, :] = current[q]
    for k in range(owners):
        state_refs[k][...] = states[lax.rem(me + k, owners)]


def chain(got):
    owners = len(got)
    per_owner = got[0].shape[0]
    block = (per_owner, GROUP_DIMENSION // 2, PAIR)
    rows = per_owner * GROUP_DIMENSION
    whole = pl.BlockSpec(memory_space=pltpu.VMEM)
    out = pl.pallas_call(
        functools.partial(chain_kernel, owners),
        in_specs=[whole] * owners,
        out_specs=[whole] * (owners + 1),
        out_shape=[jax.ShapeDtypeStruct(block, F32)] * owners
        + [jax.ShapeDtypeStruct((rows, GROUP_DIMENSION), F32)],
        scratch_shapes=[
            pltpu.VMEM((owners,) + got[0].shape, F32),
            pltpu.VMEM((owners,) + block, F32),
        ],
        name="chain",
    )(*got)
    return out[:owners], out[owners]


def finish_kernel(owners, *refs):
    state_refs = refs[:owners]
    lift_high_ref, lift_low_ref, within_ref, bonus_ref, gain_ref = refs[
        owners : owners + 5
    ]
    out_ref, states = refs[owners + 5 :]
    step = pl.program_id(0)
    me = lax.axis_index("seq")
    per_owner = state_refs[0].shape[0]
    width = out_ref.shape[1]
    d = GROUP_DIMENSION

    @pl.when(step == 0)
    def _():
        for k in range(owners):
            states[lax.rem(me % owners - k + owners, owners)] = state_refs[k][...]

    lane = iota((d // 2, PAIR), 1)
    for p in range(width // PAIR):
        normed = []
        for i in range(2):
            head = (step * (width // PAIR) + p) * 2 + i
            packed = states[head // per_owner, lax.rem(head, per_owner)]
            state = split(
                stack(
                    jnp.where(lane < d, packed, 0.0),
                    jnp.where(lane >= d, packed, 0.0),
                )
            )
            at = slice(p * PAIR + i * d, p * PAIR + (i + 1) * d)
            high, low = lift_high_ref[at], lift_low_ref[at]
            result = within_ref[at] + mm3(
                state, (stack(high, high), stack(low, low))
            )
            average = jnp.mean(result, axis=0, keepdims=True)
            centered = result - average
            spread = jnp.mean(centered * centered, axis=0, keepdims=True)
            normed.append(centered * lax.rsqrt(spread + NORM_EPS))
        cut = slice(p * PAIR, (p + 1) * PAIR)
        turned = stack(*normed).T
        out_ref[:, cut] = (turned * gain_ref[:, cut] + bonus_ref[:, cut]).astype(BF16)


def finish(states, lift_high, lift_low, within, bonus, gain):
    owners = len(states)
    tokens, features = bonus.shape
    width = STEP_PAIRS * PAIR
    natural = pl.BlockSpec((tokens, width), lambda g: (0, g))
    turned = pl.BlockSpec((width, tokens), lambda g: (g, 0))
    vector = pl.BlockSpec((1, width), lambda g: (0, g))
    whole = pl.BlockSpec(memory_space=pltpu.VMEM)
    return pl.pallas_call(
        functools.partial(finish_kernel, owners),
        grid=(features // width,),
        in_specs=[whole] * owners + [turned, turned, turned, natural, vector],
        out_specs=natural,
        out_shape=jax.ShapeDtypeStruct((tokens, features), BF16),
        scratch_shapes=[pltpu.VMEM((owners,) + states[0].shape, F32)],
        name="finish",
    )(*states, lift_high, lift_low, within, bonus, gain)


def shifted(value, by, members):
    return lax.ppermute(value, "seq", [(i, (i + by) % members) for i in range(members)])


def relay_states(both, members):
    d = GROUP_DIMENSION
    local_map, local_add = both[:, :, :d], both[:, :, d:]

    def relay(_, carried):
        pairs = [(i, i + 1) for i in range(members - 1)]
        incoming = lax.ppermute(carried[1], "seq", pairs)
        moved = jnp.einsum(
            "hvk,hkj->hvj", incoming, local_map, precision=lax.Precision.HIGHEST
        )
        return (incoming, moved + local_add)

    first = (jnp.zeros_like(local_add), local_add)
    incoming, leaving = lax.fori_loop(0, members - 1, relay, first)
    here = lax.axis_index("seq")
    closing = lax.psum(jnp.where(here == members - 1, leaving, 0.0), "seq")
    closing = closing.reshape(-1, d)
    rows = closing.shape[0] // members
    final = lax.dynamic_slice_in_dim(closing, here * rows, rows, 0)
    packed = jnp.concatenate([incoming[:, : d // 2], incoming[:, d // 2 :]], axis=2)
    return packed, final


def on_device(reader, fade, key, value, removal, rate, extra, gain):
    members = lax.axis_size("seq")
    features = reader.shape[2]
    heads = features // GROUP_DIMENSION
    owners = members if heads % members == 0 else 1
    sends, parts = local_pass(
        owners,
        reader[0],
        fade[0],
        key[0],
        value[0],
        removal[0],
        rate[0],
        extra.reshape(1, features),
    )
    if owners > 1:
        got = [sends[0]] + [shifted(sends[k], k, members) for k in range(1, owners)]
        states, final = chain(got)
        states = [states[0]] + [
            shifted(states[k], k, members) for k in range(1, owners)
        ]
    else:
        packed, final = relay_states(sends[0], members)
        states = [packed]
    blended = finish(states, *parts, gain.reshape(1, features))
    return (blended[None], final[None])


def solution(mesh):
    tokens = P(("groups", "dp"), "seq", None)
    return jax.shard_map(
        on_device,
        mesh=mesh,
        in_specs=(tokens,) * 6 + (P(), P()),
        out_specs=(tokens, tokens),
        check_vma=False,
    )
```

```python
import functools

import jax
import jax.numpy as jnp
from jax import lax
from jax.experimental import pallas as pl
from jax.experimental.pallas import tpu as pltpu
from jax.sharding import PartitionSpec as P

GROUP_DIMENSION = 64
PAIR = 2 * GROUP_DIMENSION
KEY_EPS = 1e-05
NORM_EPS = 0.00064
STEP_PAIRS = 5

F32 = jnp.float32
BF16 = jnp.bfloat16


def mm(left, right):
    return jnp.dot(left, right, preferred_element_type=F32)


def split(x):
    high = x.astype(BF16)
    return high, (x - high.astype(F32)).astype(BF16)


def side(*parts):
    return jnp.concatenate(parts, axis=1)


def stack(*parts):
    return jnp.concatenate(parts, axis=0)


def mm3(left, right):
    lh, ll = left
    rh, rl = right
    return mm(side(lh, ll), stack(rh, rh)) + mm(lh, rl)


def iota(shape, axis):
    return lax.broadcasted_iota(jnp.int32, shape, axis)


def group_ones():
    same = (iota((PAIR, PAIR), 0) // GROUP_DIMENSION) == (
        iota((PAIR, PAIR), 1) // GROUP_DIMENSION
    )
    ones = same.astype(F32).astype(BF16)
    return stack(ones, ones)


def group_sums(x, ones):
    parts = []
    for p in range(x.shape[1] // PAIR):
        high, low = split(x[:, p * PAIR : (p + 1) * PAIR])
        parts.append(mm(side(high, low), ones))
    return side(*parts)


def block_diagonal(x):
    top, bottom = x[:GROUP_DIMENSION], x[GROUP_DIMENSION:]
    none = jnp.zeros_like(top)
    return stack(side(top, none), side(none, bottom))


def product(left, right):
    rows = side(*right)
    full = mm(side(*left), stack(rows, rows))
    return full[:, :PAIR] + full[:, PAIR:]


def scores(late, away, keys, query):
    half = away[0].shape[0] // 2
    qh, ql = (block_diagonal(q) for q in query)
    early_rows = tuple(stack(a[:half], k[:half]) for a, k in zip(away, keys))
    late_rows = tuple(stack(a[half:], k[half:]) for a, k in zip(away, keys))
    early = mm3(early_rows, (qh, ql))
    later = mm3(late_rows, (qh * late, ql * late))
    return stack(early[:half], later[:half]), stack(early[half:], later[half:])


def late_columns(tokens):
    lane = iota((PAIR, 2 * tokens), 1) % tokens
    return (lane >= tokens // 2).astype(F32).astype(BF16)


def cumulative(log_step):
    tokens = log_step.shape[0]
    shape = (tokens, tokens)
    lower = (iota(shape, 0) >= iota(shape, 1)).astype(F32).astype(BF16)
    high, low = split(log_step)
    lowest = (log_step - high.astype(F32) - low.astype(F32)).astype(BF16)
    return mm(side(lower, lower), stack(high, low)) + mm(lower, lowest)


def key_side(fade_ref, removal_ref, rate_ref, key_ref, ones):
    half = fade_ref.shape[0] // 2
    log_step = -jnp.exp(fade_ref[...].astype(F32))
    cum = cumulative(log_step)
    middle = cum[half - 1 : half]
    removal = removal_ref[...].astype(F32)
    norm = group_sums(removal * removal, ones) * (1.0 / GROUP_DIMENSION)
    kappa = removal * lax.rsqrt(norm + KEY_EPS) * GROUP_DIMENSION ** (-0.5)
    inverse = jnp.exp(middle - cum)
    away = kappa * rate_ref[...].astype(F32) * inverse
    keys = key_ref[...].astype(F32) * inverse
    return log_step, cum, middle, kappa, away, keys


def range_kernel(
    owners, fade_ref, key_ref, value_ref, removal_ref, rate_ref, *rest
):
    send_refs = rest[:owners]
    solved_ref, held, sems = rest[owners:]
    step = pl.program_id(0)
    me = lax.axis_index("seq")
    tokens, width = fade_ref.shape
    pairs = width // PAIR
    per_owner = held.shape[1]
    d = GROUP_DIMENSION

    ones = group_ones()
    late = late_columns(tokens)
    strict = iota((tokens, tokens), 0) < iota((tokens, tokens), 1)
    log_step, cum, middle, kappa, away, keys = key_side(
        fade_ref, removal_ref, rate_ref, key_ref, ones
    )
    end = cum[tokens - 1 : tokens]
    before = cum - log_step
    to_end = jnp.exp(end - middle)
    gamma_end = jnp.exp(end)
    toward_mid = -kappa * jnp.exp(before - middle)
    toward_abs = -kappa * jnp.exp(before)
    value = value_ref[...].astype(F32)

    cuts = [slice(p * PAIR, (p + 1) * PAIR) for p in range(pairs)]
    solved, powers, twice = [], [], []
    for cut in cuts:
        mix_away, mix_keys = scores(
            late, split(away[:, cut]), split(keys[:, cut]), split(toward_mid[:, cut].T)
        )
        start = toward_abs[:, cut].T
        value_t = value[:, cut].T.astype(BF16)
        for i in range(2):
            lanes = slice(i * tokens, (i + 1) * tokens)
            rows = slice(i * d, (i + 1) * d)
            values = side(value_t[rows], value_t[rows])
            mixed = split(jnp.where(strict, mix_keys[:, lanes], 0.0))
            solved.append(stack(start[rows], mm(values, stack(*mixed))))
            powers.append(jnp.where(strict, mix_away[:, lanes], 0.0))
            twice.append(values)

    for h in range(2 * pairs):
        ps = split(powers[h])
        out = product(tuple(stack(w, q) for w, q in zip(split(solved[h]), ps)), ps)
        solved[h] = solved[h] + out[:tokens]
        powers[h] = out[tokens:].astype(BF16)
    both = [side(*solved[2 * p : 2 * p + 2]) for p in range(pairs)]
    none = jnp.zeros((tokens, tokens), BF16)
    reach = 2
    while reach < tokens:
        for p in range(pairs):
            one, two = powers[2 * p : 2 * p + 2]
            factor = stack(side(one, none), side(none, two))
            left = both[p].astype(BF16)
            if reach * 2 < tokens:
                out = mm(stack(left, side(one, two)), factor)
                square = out[tokens:].astype(BF16)
                powers[2 * p] = square[:, :tokens]
                powers[2 * p + 1] = square[:, tokens:]
                both[p] = both[p] + out[:tokens]
            else:
                both[p] = both[p] + mm(left, factor)
        reach *= 2

    lane = iota((d, PAIR), 1)
    sub = iota((d, PAIR), 0)
    for p, cut in enumerate(cuts):
        away_end = split(away[:, cut] * to_end[:, cut])
        keys_end = split(keys[:, cut] * to_end[:, cut])
        for i in range(2):
            ws = split(both[p][:, i * tokens : (i + 1) * tokens])
            solved_ref[2 * p + i] = side(*ws)
            ended = product(ws, away_end)
            stay = jnp.where(lane == sub + i * d, gamma_end[:, cut], 0.0)
            state_map = ended[:d] + stay
            state_add = ended[d:] + mm(twice[2 * p + i], stack(*keys_end))
            if i == 0:
                state_add = pltpu.roll(state_add, d, 1)
            else:
                state_map = pltpu.roll(state_map, d, 1)
            head = (step * pairs + p) * 2 + i
            slot = lax.rem(head // per_owner - me % owners + owners, owners)
            held[slot, lax.rem(head, per_owner)] = jnp.where(
                lane < d, state_map, state_add
            )

    @pl.when(step == pl.num_programs(0) - 1)
    def _():
        copies = [
            pltpu.make_async_copy(held.at[k], send_refs[k], sems.at[k])
            for k in range(owners)
        ]
        for copy in copies:
            copy.start()
        for copy in copies:
            copy.wait()


def specs(tokens, features):
    width = STEP_PAIRS * PAIR
    natural = pl.BlockSpec((tokens, width), lambda g: (0, g))
    turned = pl.BlockSpec((width, tokens), lambda g: (g, 0))
    vector = pl.BlockSpec((1, width), lambda g: (0, g))
    solved = pl.BlockSpec((2 * STEP_PAIRS, tokens, 2 * tokens), lambda g: (g, 0, 0))
    return (features // width,), natural, turned, vector, solved


def range_pass(owners, fade, key, value, removal, rate):
    tokens, features = fade.shape
    heads = features // GROUP_DIMENSION
    grid, natural, _, _, solved = specs(tokens, features)
    block = (heads // owners, GROUP_DIMENSION, PAIR)
    out = pl.pallas_call(
        functools.partial(range_kernel, owners),
        grid=grid,
        in_specs=[natural] * 5,
        out_specs=[pl.BlockSpec(memory_space=pl.ANY)] * owners + [solved],
        out_shape=[jax.ShapeDtypeStruct(block, F32)] * owners
        + [jax.ShapeDtypeStruct((heads, tokens, 2 * tokens), BF16)],
        scratch_shapes=[
            pltpu.VMEM((owners,) + block, F32),
            pltpu.SemaphoreType.DMA((owners,)),
        ],
        name="range_pass",
    )(fade, key, value, removal, rate)
    return out[:owners], out[owners]


def read_kernel(
    reader_ref,
    fade_ref,
    key_ref,
    value_ref,
    removal_ref,
    rate_ref,
    extra_ref,
    solved_ref,
    lift_high_ref,
    lift_low_ref,
    within_ref,
    bonus_ref,
):
    tokens, width = fade_ref.shape
    d = GROUP_DIMENSION
    ones = group_ones()
    late = late_columns(tokens)
    seen = iota((tokens, tokens), 0) <= iota((tokens, tokens), 1)
    _, cum, middle, _, away, keys = key_side(
        fade_ref, removal_ref, rate_ref, key_ref, ones
    )
    reader = reader_ref[...].astype(F32)
    value = value_ref[...].astype(F32)
    bonus = group_sums(reader * key_ref[...].astype(F32) * extra_ref[...], ones)
    bonus_ref[...] = bonus * value
    reader_mid = reader * jnp.exp(cum - middle)
    reader_abs = reader * jnp.exp(cum)

    for p in range(width // PAIR):
        cut = slice(p * PAIR, (p + 1) * PAIR)
        read_away, read_keys = scores(
            late, split(away[:, cut]), split(keys[:, cut]), split(reader_mid[:, cut].T)
        )
        start = reader_abs[:, cut].T
        value_t = value[:, cut].T.astype(BF16)
        for i in range(2):
            lanes = slice(i * tokens, (i + 1) * tokens)
            rows = slice(i * d, (i + 1) * d)
            at = slice(p * PAIR + i * d, p * PAIR + (i + 1) * d)
            both = solved_ref[2 * p + i]
            solved = both[:, :tokens], both[:, tokens:]
            values = side(value_t[rows], value_t[rows])
            read = product(solved, split(jnp.where(seen, read_away[:, lanes], 0.0)))
            direct = split(jnp.where(seen, read_keys[:, lanes], 0.0))
            within_ref[at] = read[d:] + mm(values, stack(*direct))
            lift_high_ref[at], lift_low_ref[at] = split(start[rows] + read[:d])


def read_pass(reader, fade, key, value, removal, rate, extra, solved):
    tokens, features = reader.shape
    grid, natural, turned, vector, solved_spec = specs(tokens, features)
    return pl.pallas_call(
        read_kernel,
        grid=grid,
        in_specs=[natural] * 6 + [vector, solved_spec],
        out_specs=[turned, turned, turned, natural],
        out_shape=[
            jax.ShapeDtypeStruct((features, tokens), BF16),
            jax.ShapeDtypeStruct((features, tokens), BF16),
            jax.ShapeDtypeStruct((features, tokens), F32),
            jax.ShapeDtypeStruct((tokens, features), F32),
        ],
        name="read_pass",
    )(reader, fade, key, value, removal, rate, extra, solved)


def pack_rows(state):
    rows = state.shape[0] // 2
    return side(state[:rows], state[rows:])


def chain_kernel(owners, *refs):
    got_refs = refs[:owners]
    state_refs = refs[owners : 2 * owners]
    final_ref, ranges, states = refs[2 * owners :]
    me = lax.axis_index("seq")
    per_owner = got_refs[0].shape[0]
    for k in range(owners):
        ranges[lax.rem(me - k + owners, owners)] = got_refs[k][...]
    d = GROUP_DIMENSION
    current = []
    for q in range(per_owner):
        states[0, q] = jnp.zeros((d // 2, PAIR), F32)
        current.append(ranges[0, q][:, d:])
    for i in range(1, owners + 1):
        for q in range(per_owner):
            if i < owners:
                states[i, q] = pack_rows(current[q])
                both = ranges[i, q]
                maps = split(both)
                moved = mm3(split(current[q]), maps)[:, :d]
                current[q] = moved + both[:, d:]
            else:
                final_ref[q * d : (q + 1) * d, :] = current[q]
    for k in range(owners):
        state_refs[k][...] = states[lax.rem(me + k, owners)]


def chain(got):
    owners = len(got)
    per_owner = got[0].shape[0]
    block = (per_owner, GROUP_DIMENSION // 2, PAIR)
    rows = per_owner * GROUP_DIMENSION
    whole = pl.BlockSpec(memory_space=pltpu.VMEM)
    out = pl.pallas_call(
        functools.partial(chain_kernel, owners),
        in_specs=[whole] * owners,
        out_specs=[whole] * (owners + 1),
        out_shape=[jax.ShapeDtypeStruct(block, F32)] * owners
        + [jax.ShapeDtypeStruct((rows, GROUP_DIMENSION), F32)],
        scratch_shapes=[
            pltpu.VMEM((owners,) + got[0].shape, F32),
            pltpu.VMEM((owners,) + block, F32),
        ],
        name="chain",
    )(*got)
    return out[:owners], out[owners]


def finish_kernel(owners, *refs):
    state_refs = refs[:owners]
    lift_high_ref, lift_low_ref, within_ref, bonus_ref, gain_ref = refs[
        owners : owners + 5
    ]
    out_ref, states = refs[owners + 5 :]
    step = pl.program_id(0)
    me = lax.axis_index("seq")
    per_owner = state_refs[0].shape[0]
    width = out_ref.shape[1]
    d = GROUP_DIMENSION

    @pl.when(step == 0)
    def _():
        for k in range(owners):
            states[lax.rem(me % owners - k + owners, owners)] = state_refs[k][...]

    lane = iota((d // 2, PAIR), 1)
    for p in range(width // PAIR):
        normed = []
        for i in range(2):
            head = (step * (width // PAIR) + p) * 2 + i
            packed = states[head // per_owner, lax.rem(head, per_owner)]
            state = split(
                stack(
                    jnp.where(lane < d, packed, 0.0),
                    jnp.where(lane >= d, packed, 0.0),
                )
            )
            at = slice(p * PAIR + i * d, p * PAIR + (i + 1) * d)
            high, low = lift_high_ref[at], lift_low_ref[at]
            result = within_ref[at] + mm3(
                state, (stack(high, high), stack(low, low))
            )
            average = jnp.mean(result, axis=0, keepdims=True)
            centered = result - average
            spread = jnp.mean(centered * centered, axis=0, keepdims=True)
            normed.append(centered * lax.rsqrt(spread + NORM_EPS))
        cut = slice(p * PAIR, (p + 1) * PAIR)
        turned = stack(*normed).T
        out_ref[:, cut] = (turned * gain_ref[:, cut] + bonus_ref[:, cut]).astype(BF16)


def finish(states, lift_high, lift_low, within, bonus, gain):
    owners = len(states)
    tokens, features = bonus.shape
    grid, natural, turned, vector, _ = specs(tokens, features)
    whole = pl.BlockSpec(memory_space=pltpu.VMEM)
    return pl.pallas_call(
        functools.partial(finish_kernel, owners),
        grid=grid,
        in_specs=[whole] * owners + [turned, turned, turned, natural, vector],
        out_specs=natural,
        out_shape=jax.ShapeDtypeStruct((tokens, features), BF16),
        scratch_shapes=[pltpu.VMEM((owners,) + states[0].shape, F32)],
        name="finish",
    )(*states, lift_high, lift_low, within, bonus, gain)


def shifted(value, by, members):
    return lax.ppermute(value, "seq", [(i, (i + by) % members) for i in range(members)])


def relay_states(both, members):
    d = GROUP_DIMENSION
    local_map, local_add = both[:, :, :d], both[:, :, d:]

    def relay(_, carried):
        pairs = [(i, i + 1) for i in range(members - 1)]
        incoming = lax.ppermute(carried[1], "seq", pairs)
        moved = jnp.einsum(
            "hvk,hkj->hvj", incoming, local_map, precision=lax.Precision.HIGHEST
        )
        return (incoming, moved + local_add)

    first = (jnp.zeros_like(local_add), local_add)
    incoming, leaving = lax.fori_loop(0, members - 1, relay, first)
    here = lax.axis_index("seq")
    closing = lax.psum(jnp.where(here == members - 1, leaving, 0.0), "seq")
    closing = closing.reshape(-1, d)
    rows = closing.shape[0] // members
    final = lax.dynamic_slice_in_dim(closing, here * rows, rows, 0)
    packed = jnp.concatenate([incoming[:, : d // 2], incoming[:, d // 2 :]], axis=2)
    return packed, final


def on_device(reader, fade, key, value, removal, rate, extra, gain):
    members = lax.axis_size("seq")
    features = reader.shape[2]
    heads = features // GROUP_DIMENSION
    owners = members if heads % members == 0 else 1
    keyed = (fade[0], key[0], value[0], removal[0], rate[0])
    sends, solved = range_pass(owners, *keyed)
    parts = read_pass(reader[0], *keyed, extra.reshape(1, features), solved)
    if owners > 1:
        got = [sends[0]] + [shifted(sends[k], k, members) for k in range(1, owners)]
        got, parts = lax.optimization_barrier((got, parts))
        states, final = chain(got)
        states = [states[0]] + [
            shifted(states[k], k, members) for k in range(1, owners)
        ]
    else:
        packed, final = relay_states(sends[0], members)
        states = [packed]
    blended = finish(states, *parts, gain.reshape(1, features))
    return (blended[None], final[None])


def solution(mesh):
    tokens = P(("groups", "dp"), "seq", None)
    return jax.shard_map(
        on_device,
        mesh=mesh,
        in_specs=(tokens,) * 6 + (P(), P()),
        out_specs=(tokens, tokens),
        check_vma=False,
    )
```

```python
import functools

import jax
import jax.numpy as jnp
from jax import lax
from jax.experimental import pallas as pl
from jax.experimental.pallas import tpu as pltpu
from jax.sharding import PartitionSpec as P

GROUP_DIMENSION = 64
PAIR = 2 * GROUP_DIMENSION
KEY_EPS = 1e-05
NORM_EPS = 0.00064

F32 = jnp.float32
BF16 = jnp.bfloat16


def mm(left, right):
    return jnp.dot(left, right, preferred_element_type=F32)


def split(x):
    high = x.astype(BF16)
    return high, (x - high.astype(F32)).astype(BF16)


def side(*parts):
    return jnp.concatenate(parts, axis=1)


def stack(*parts):
    return jnp.concatenate(parts, axis=0)


def mm3(left, right):
    lh, ll = left
    rh, rl = right
    return mm(side(lh, ll), stack(rh, rh)) + mm(lh, rl)


def iota(shape, axis):
    return lax.broadcasted_iota(jnp.int32, shape, axis)


def group_ones():
    same = (iota((PAIR, PAIR), 0) // GROUP_DIMENSION) == (
        iota((PAIR, PAIR), 1) // GROUP_DIMENSION
    )
    ones = same.astype(F32).astype(BF16)
    return stack(ones, ones)


def group_sums(x, ones):
    parts = []
    for p in range(x.shape[1] // PAIR):
        high, low = split(x[:, p * PAIR : (p + 1) * PAIR])
        parts.append(mm(side(high, low), ones))
    return side(*parts)


def block_diagonal(x):
    top, bottom = x[:GROUP_DIMENSION], x[GROUP_DIMENSION:]
    none = jnp.zeros_like(top)
    return stack(side(top, none), side(none, bottom))


def folded(left, right):
    full = mm(left, right)
    return full[:, :PAIR] + full[:, PAIR:]


def lane_blocks(x, low, high):
    parts = []
    for i in range(2):
        one = x[:, i * PAIR : (i + 1) * PAIR]
        none = jnp.zeros_like(one)
        for mask in (low, high):
            kept = one * mask
            parts.append(side(kept, none) if i == 0 else side(none, kept))
    return stack(*parts)


def scores(late, away, keys, query, terms):
    half = away[0].shape[0] // 2
    qh, ql = (block_diagonal(q) for q in query)

    def against(part, high, low):
        left = [stack(a[part], k[part]) for a, k in zip(away, keys)]
        out = mm(side(*left), stack(high, high))
        return out + mm(left[0], low) if terms == 3 else out

    early = against(slice(0, half), qh, ql)
    later = against(slice(half, 2 * half), qh * late, ql * late)
    return early, later


def late_columns(tokens):
    lane = iota((PAIR, 2 * tokens), 1) % tokens
    return (lane >= tokens // 2).astype(F32).astype(BF16)


def cumulative(log_step):
    tokens = log_step.shape[0]
    shape = (tokens, tokens)
    lower = (iota(shape, 0) >= iota(shape, 1)).astype(F32).astype(BF16)
    high, low = split(log_step)
    lowest = (log_step - high.astype(F32) - low.astype(F32)).astype(BF16)
    return mm(side(lower, lower), stack(high, low)) + mm(lower, lowest)


def key_side(fade_ref, removal_ref, rate_ref, key_ref, ones, ready=lambda k: None):
    half = fade_ref.shape[0] // 2
    ready(0)
    log_step = -jnp.exp(fade_ref[...].astype(F32))
    cum = cumulative(log_step)
    middle = cum[half - 1 : half]
    inverse = jnp.exp(middle - cum)
    ready(1)
    removal = removal_ref[...].astype(F32)
    norm = group_sums(removal * removal, ones) * (1.0 / GROUP_DIMENSION)
    kappa = removal * lax.rsqrt(norm + KEY_EPS) * GROUP_DIMENSION ** (-0.5)
    ready(2)
    away = kappa * rate_ref[...].astype(F32) * inverse
    ready(3)
    keys = key_ref[...].astype(F32) * inverse
    return log_step, cum, middle, kappa, away, keys


def range_kernel(
    owners, fade_hbm, key_hbm, value_hbm, removal_hbm, rate_hbm, *rest
):
    send_refs = rest[:owners]
    solved_ref, loaded, held, load_sems, sems = rest[owners:]
    sources = (fade_hbm, removal_hbm, rate_hbm, key_hbm, value_hbm)
    loads = [
        pltpu.make_async_copy(source, loaded.at[k], load_sems.at[k])
        for k, source in enumerate(sources)
    ]
    for load in loads:
        load.start()
    fade_ref, removal_ref, rate_ref, key_ref, value_ref = (
        loaded.at[k] for k in range(len(sources))
    )
    me = lax.axis_index("seq")
    tokens, width = fade_ref.shape
    pairs = width // PAIR
    per_owner = held.shape[1]
    d = GROUP_DIMENSION

    ones = group_ones()
    late = late_columns(tokens)
    log_step, cum, middle, kappa, away, keys = key_side(
        fade_ref, removal_ref, rate_ref, key_ref, ones, lambda k: loads[k].wait()
    )
    loads[4].wait()
    end = cum[tokens - 1 : tokens]
    before = cum - log_step
    to_end = jnp.exp(end - middle)
    gamma_end = jnp.exp(end)
    toward_mid = -kappa * jnp.exp(before - middle)
    toward_abs = -kappa * jnp.exp(before)
    value = value_ref[...].astype(F32)

    cuts = [slice(p * PAIR, (p + 1) * PAIR) for p in range(pairs)]
    block = iota((d, 2 * PAIR), 1) % PAIR
    is_low = block < d
    strict = iota((d, 2 * PAIR), 0) < block % d
    low = (iota((d, PAIR), 1) < d).astype(F32).astype(BF16)
    high = (iota((d, PAIR), 1) >= d).astype(F32).astype(BF16)

    known, values, within, across, powers = [], [], [], [], []
    for cut in cuts:
        early, later = scores(
            late,
            split(away[:, cut]),
            split(keys[:, cut]),
            split(toward_mid[:, cut].T),
            2,
        )
        mix_early, mix_later = early[:d], later[:d]
        power = jnp.where(strict, jnp.where(is_low, mix_early, mix_later), 0.0)
        within.append(power)
        powers.append(power.astype(BF16))
        across.append(jnp.where(is_low, 0.0, mix_early))
        key_early, key_later = early[d:], later[d:]
        key_early = jnp.where(is_low & ~strict, 0.0, key_early)
        key_later = jnp.where(~is_low & strict, key_later, 0.0)
        mixed = stack(key_early.astype(BF16), key_later.astype(BF16))
        none = jnp.zeros((tokens, tokens), BF16)
        mixed = stack(side(mixed[:, :tokens], none), side(none, mixed[:, tokens:]))
        start = toward_abs[:, cut].T
        value_t = value[:, cut].T.astype(BF16)
        moved = mm(side(value_t[:d], value_t[d:]), mixed)
        known.append(stack(side(start[:d], start[d:]), moved))
        values.append(value_t)

    reach = 1
    while reach < d:
        for p in range(pairs):
            factor = lane_blocks(powers[p], low, high)
            if reach == 1:
                powers[p] = mm(powers[p], factor).astype(BF16)
            elif reach * 2 < d:
                out = mm(stack(within[p].astype(BF16), powers[p]), factor)
                within[p] = within[p] + powers[p].astype(F32) + out[:d]
                powers[p] = out[d:].astype(BF16)
            else:
                out = mm(within[p].astype(BF16), factor)
                within[p] = within[p] + powers[p].astype(F32) + out
        reach *= 2
    solved = []
    for p in range(pairs):
        factor = lane_blocks(within[p].astype(BF16), low, high)
        left = stack(known[p].astype(BF16), across[p].astype(BF16))
        out = mm(left, factor)
        solved.append(known[p] + out[:tokens])
        across[p] = (across[p] + out[tokens:]).astype(BF16)
    for p in range(pairs):
        one, two = across[p][:, :PAIR], across[p][:, PAIR:]
        none = jnp.zeros_like(one)
        factor = stack(side(one, none), side(none, none), side(none, two), side(none, none))
        solved[p] = (solved[p] + mm(solved[p].astype(BF16), factor)).astype(BF16)

    lane = iota((d, PAIR), 1)
    sub = iota((d, PAIR), 0)
    none = jnp.zeros((d, PAIR), BF16)
    for p, cut in enumerate(cuts):
        away_end = side(*split(away[:, cut] * to_end[:, cut]))
        keys_end = side(*split(keys[:, cut] * to_end[:, cut]))
        lefts = [
            side(
                solved[p][:, i * tokens : (i + 1) * tokens],
                stack(none, values[p][i * d : (i + 1) * d]),
            )
            for i in range(2)
        ]
        ended = folded(stack(*lefts), stack(away_end, keys_end))
        for i in range(2):
            solved_ref[2 * p + i] = lefts[i]
            stay = jnp.where(lane == sub + i * d, gamma_end[:, cut], 0.0)
            state_map = ended[2 * i * d : (2 * i + 1) * d] + stay
            state_add = ended[(2 * i + 1) * d : (2 * i + 2) * d]
            if i == 0:
                state_add = pltpu.roll(state_add, d, 1)
            else:
                state_map = pltpu.roll(state_map, d, 1)
            head = 2 * p + i
            slot = lax.rem(head // per_owner - me % owners + owners, owners)
            held[slot, head % per_owner] = jnp.where(
                lane < d, state_map, state_add
            )

    copies = [
        pltpu.make_async_copy(held.at[k], send_refs[k], sems.at[k])
        for k in range(owners)
    ]
    for copy in copies:
        copy.start()
    for copy in copies:
        copy.wait()


def resident(count):
    return [pl.BlockSpec(memory_space=pltpu.VMEM)] * count


def limit(mib):
    return pltpu.CompilerParams(vmem_limit_bytes=mib << 20)


def range_pass(owners, fade, key, value, removal, rate):
    tokens, features = fade.shape
    heads = features // GROUP_DIMENSION
    block = (heads // owners, GROUP_DIMENSION, PAIR)
    out = pl.pallas_call(
        functools.partial(range_kernel, owners),
        in_specs=[pl.BlockSpec(memory_space=pltpu.HBM)] * 5,
        out_specs=[pl.BlockSpec(memory_space=pl.ANY)] * owners + resident(2),
        out_shape=[jax.ShapeDtypeStruct(block, F32)] * owners
        + [
            jax.ShapeDtypeStruct((heads, tokens, 2 * tokens), BF16),
            jax.ShapeDtypeStruct((5, tokens, features), BF16),
        ],
        scratch_shapes=[
            pltpu.VMEM((owners,) + block, F32),
            pltpu.SemaphoreType.DMA((5,)),
            pltpu.SemaphoreType.DMA((owners,)),
        ],
        compiler_params=limit(40),
        name="range_pass",
    )(fade, key, value, removal, rate)
    return out[:owners], out[owners:]


def read_kernel(
    reader_ref,
    extra_ref,
    solved_ref,
    loaded,
    lift_high_ref,
    lift_low_ref,
    within_ref,
    bonus_ref,
):
    fade_ref, removal_ref, rate_ref, key_ref, value_ref = (
        loaded.at[k] for k in range(loaded.shape[0])
    )
    tokens, width = fade_ref.shape
    d = GROUP_DIMENSION
    ones = group_ones()
    late = late_columns(tokens)
    seen = iota((tokens, tokens), 0) <= iota((tokens, tokens), 1)
    _, cum, middle, _, away, keys = key_side(
        fade_ref, removal_ref, rate_ref, key_ref, ones
    )
    reader = reader_ref[...].astype(F32)
    value = value_ref[...].astype(F32)
    bonus = group_sums(reader * key_ref[...].astype(F32) * extra_ref[...], ones)
    bonus_ref[...] = bonus * value
    reader_mid = reader * jnp.exp(cum - middle)
    reader_abs = reader * jnp.exp(cum)

    for p in range(width // PAIR):
        cut = slice(p * PAIR, (p + 1) * PAIR)
        early, later = scores(
            late,
            split(away[:, cut]),
            split(keys[:, cut]),
            split(reader_mid[:, cut].T),
            3,
        )
        start = reader_abs[:, cut].T
        for i in range(2):
            lanes = slice(i * tokens, (i + 1) * tokens)
            rows = slice(i * d, (i + 1) * d)
            at = slice(p * PAIR + i * d, p * PAIR + (i + 1) * d)

            def read(part):
                whole = stack(early[part, lanes], later[part, lanes])
                return side(*split(jnp.where(seen, whole, 0.0)))

            out = folded(
                solved_ref[2 * p + i], stack(read(slice(0, d)), read(slice(d, 2 * d)))
            )
            within_ref[at] = out[d:]
            lift_high_ref[at], lift_low_ref[at] = split(start[rows] + out[:d])


def read_pass(reader, extra, solved, loaded):
    tokens, features = reader.shape
    return pl.pallas_call(
        read_kernel,
        in_specs=resident(4),
        out_specs=resident(4),
        out_shape=[
            jax.ShapeDtypeStruct((features, tokens), BF16),
            jax.ShapeDtypeStruct((features, tokens), BF16),
            jax.ShapeDtypeStruct((features, tokens), F32),
            jax.ShapeDtypeStruct((tokens, features), F32),
        ],
        compiler_params=limit(40),
        name="read_pass",
    )(reader, extra, solved, loaded)


def chain_kernel(owners, *refs):
    got_refs = refs[:owners]
    state_refs = refs[owners : 2 * owners]
    final_ref, ranges, states = refs[2 * owners :]
    me = lax.axis_index("seq")
    per_owner = got_refs[0].shape[0]
    for k in range(owners):
        ranges[lax.rem(me - k + owners, owners)] = got_refs[k][...]
    d = GROUP_DIMENSION
    lane = iota((d // 2, PAIR), 1)
    none = jnp.zeros((d, 2 * PAIR), BF16)
    current = []
    for q in range(per_owner):
        states[0, q] = jnp.zeros((d // 2, PAIR), F32)
        current.append(ranges[0, q])
    for i in range(1, owners):
        for q in range(per_owner):
            now = current[q]
            states[i, q] = jnp.where(
                lane < d, pltpu.roll(now[: d // 2], d, 1), now[d // 2 :]
            )
            both = ranges[i, q]
            maps = side(*split(pltpu.roll(both, d, 1)))
            out = mm(stack(*split(now)), stack(none, maps))
            current[q] = out[:d, :PAIR] + out[:d, PAIR:] + out[d:, :PAIR] + both
    for q in range(per_owner):
        final_ref[q * d : (q + 1) * d, :] = pltpu.roll(current[q], d, 1)[:, :d]
    for k in range(owners):
        state_refs[k][...] = states[lax.rem(me + k, owners)]


def chain(got):
    owners = len(got)
    per_owner = got[0].shape[0]
    block = (per_owner, GROUP_DIMENSION // 2, PAIR)
    rows = per_owner * GROUP_DIMENSION
    out = pl.pallas_call(
        functools.partial(chain_kernel, owners),
        in_specs=resident(owners),
        out_specs=resident(owners + 1),
        out_shape=[jax.ShapeDtypeStruct(block, F32)] * owners
        + [jax.ShapeDtypeStruct((rows, GROUP_DIMENSION), F32)],
        scratch_shapes=[
            pltpu.VMEM((owners,) + got[0].shape, F32),
            pltpu.VMEM((owners,) + block, F32),
        ],
        compiler_params=limit(40),
        name="chain",
    )(*got)
    return out[:owners], out[owners]


def finish_kernel(owners, *refs):
    state_refs = refs[:owners]
    lift_high_ref, lift_low_ref, within_ref, bonus_ref, gain_ref = refs[
        owners : owners + 5
    ]
    out_ref, states = refs[owners + 5 :]
    me = lax.axis_index("seq")
    per_owner = state_refs[0].shape[0]
    width = out_ref.shape[1]
    d = GROUP_DIMENSION

    for k in range(owners):
        states[lax.rem(me % owners - k + owners, owners)] = state_refs[k][...]

    lane = iota((d // 2, PAIR), 1)
    for p in range(width // PAIR):
        normed = []
        for i in range(2):
            head = 2 * p + i
            packed = states[head // per_owner, head % per_owner]
            state = split(
                stack(
                    jnp.where(lane < d, packed, 0.0),
                    jnp.where(lane >= d, packed, 0.0),
                )
            )
            at = slice(p * PAIR + i * d, p * PAIR + (i + 1) * d)
            high, low = lift_high_ref[at], lift_low_ref[at]
            result = within_ref[at] + mm3(
                state, (stack(high, high), stack(low, low))
            )
            average = jnp.mean(result, axis=0, keepdims=True)
            centered = result - average
            spread = jnp.mean(centered * centered, axis=0, keepdims=True)
            normed.append(centered * lax.rsqrt(spread + NORM_EPS))
        cut = slice(p * PAIR, (p + 1) * PAIR)
        turned = stack(*normed).T
        out_ref[:, cut] = (turned * gain_ref[:, cut] + bonus_ref[:, cut]).astype(BF16)


def finish(states, lift_high, lift_low, within, bonus, gain):
    owners = len(states)
    tokens, features = bonus.shape
    return pl.pallas_call(
        functools.partial(finish_kernel, owners),
        in_specs=resident(owners + 5),
        out_specs=resident(1)[0],
        out_shape=jax.ShapeDtypeStruct((tokens, features), BF16),
        scratch_shapes=[pltpu.VMEM((owners,) + states[0].shape, F32)],
        compiler_params=limit(40),
        name="finish",
    )(*states, lift_high, lift_low, within, bonus, gain)


def shifted(value, by, members):
    return lax.ppermute(value, "seq", [(i, (i + by) % members) for i in range(members)])


def relay_states(both, members):
    d = GROUP_DIMENSION
    local_map, local_add = both[:, :, :d], both[:, :, d:]

    def relay(_, carried):
        pairs = [(i, i + 1) for i in range(members - 1)]
        incoming = lax.ppermute(carried[1], "seq", pairs)
        moved = jnp.einsum(
            "hvk,hkj->hvj", incoming, local_map, precision=lax.Precision.HIGHEST
        )
        return (incoming, moved + local_add)

    first = (jnp.zeros_like(local_add), local_add)
    incoming, leaving = lax.fori_loop(0, members - 1, relay, first)
    here = lax.axis_index("seq")
    closing = lax.psum(jnp.where(here == members - 1, leaving, 0.0), "seq")
    closing = closing.reshape(-1, d)
    rows = closing.shape[0] // members
    final = lax.dynamic_slice_in_dim(closing, here * rows, rows, 0)
    packed = jnp.concatenate([incoming[:, : d // 2], incoming[:, d // 2 :]], axis=2)
    return packed, final


def on_device(reader, fade, key, value, removal, rate, extra, gain):
    members = lax.axis_size("seq")
    features = reader.shape[2]
    heads = features // GROUP_DIMENSION
    owners = members if heads % members == 0 else 1
    keyed = (fade[0], key[0], value[0], removal[0], rate[0])
    keyed = [pltpu.with_memory_space_constraint(x, pltpu.HBM) for x in keyed]
    sends, kept = range_pass(owners, *keyed)
    parts = read_pass(reader[0], extra.reshape(1, features), *kept)
    if owners > 1:
        got = [sends[0]] + [shifted(sends[k], k, members) for k in range(1, owners)]
        got, parts = lax.optimization_barrier((got, parts))
        states, final = chain(got)
        states = [states[0]] + [
            shifted(states[k], k, members) for k in range(1, owners)
        ]
    else:
        packed, final = relay_states(sends[0], members)
        states = [packed]
    blended = finish(states, *parts, gain.reshape(1, features))
    return (blended[None], final[None])


def solution(mesh):
    tokens = P(("groups", "dp"), "seq", None)
    return jax.shard_map(
        on_device,
        mesh=mesh,
        in_specs=(tokens,) * 6 + (P(), P()),
        out_specs=(tokens, tokens),
        check_vma=False,
    )
```

```python
import functools

import jax
import jax.numpy as jnp
from jax import lax
from jax.experimental import pallas as pl
from jax.experimental.pallas import tpu as pltpu
from jax.sharding import PartitionSpec as P

GROUP_DIMENSION = 64
PAIR = 2 * GROUP_DIMENSION
KEY_EPS = 1e-05
NORM_EPS = 0.00064

F32 = jnp.float32
BF16 = jnp.bfloat16


def mm(left, right):
    return jnp.dot(left, right, preferred_element_type=F32)


def mm_turned(left, right):
    return lax.dot_general(
        left, right, (((1,), (1,)), ((), ())), preferred_element_type=F32
    )


def split(x):
    high = x.astype(BF16)
    return high, (x - high.astype(F32)).astype(BF16)


def side(*parts):
    return jnp.concatenate(parts, axis=1)


def stack(*parts):
    return jnp.concatenate(parts, axis=0)


def mm3(left, right):
    lh, ll = left
    rh, rl = right
    return mm(side(lh, ll), stack(rh, rh)) + mm(lh, rl)


def iota(shape, axis):
    return lax.broadcasted_iota(jnp.int32, shape, axis)


def group_ones():
    same = (iota((PAIR, PAIR), 0) // GROUP_DIMENSION) == (
        iota((PAIR, PAIR), 1) // GROUP_DIMENSION
    )
    ones = same.astype(F32).astype(BF16)
    return stack(ones, ones)


def group_sums(x, ones):
    parts = []
    for p in range(x.shape[1] // PAIR):
        high, low = split(x[:, p * PAIR : (p + 1) * PAIR])
        parts.append(mm(side(high, low), ones))
    return side(*parts)


def block_diagonal(x):
    top, bottom = x[:GROUP_DIMENSION], x[GROUP_DIMENSION:]
    none = jnp.zeros_like(top)
    return stack(side(top, none), side(none, bottom))


def folded(left, right):
    full = mm(left, right)
    return full[:, :PAIR] + full[:, PAIR:]


def lane_blocks(x, low, high):
    parts = []
    for i in range(2):
        one = x[:, i * PAIR : (i + 1) * PAIR]
        none = jnp.zeros_like(one)
        for mask in (low, high):
            kept = one * mask
            parts.append(side(kept, none) if i == 0 else side(none, kept))
    return stack(*parts)


def scores(late, away, keys, query, terms):
    half = away[0].shape[0] // 2
    qh, ql = (block_diagonal(q) for q in query)

    def against(part, high, low):
        left = [stack(a[part], k[part]) for a, k in zip(away, keys)]
        out = mm(side(*left), stack(high, high))
        return out + mm(left[0], low) if terms == 3 else out

    early = against(slice(0, half), qh, ql)
    later = against(slice(half, 2 * half), qh * late, ql * late)
    return early, later


def late_columns(tokens):
    lane = iota((PAIR, 2 * tokens), 1) % tokens
    return (lane >= tokens // 2).astype(F32).astype(BF16)


def cumulative(log_step):
    tokens = log_step.shape[0]
    shape = (tokens, tokens)
    lower = (iota(shape, 0) >= iota(shape, 1)).astype(F32).astype(BF16)
    return mm(side(lower, lower), stack(*split(log_step)))


def key_side(fade_ref, removal_ref, rate_ref, key_ref, ones, ready=lambda k: None):
    half = fade_ref.shape[0] // 2
    ready(0)
    log_step = -jnp.exp(fade_ref[...].astype(F32))
    cum = cumulative(log_step)
    middle = cum[half - 1 : half]
    past = cum - middle
    inverse = jnp.exp(-past)
    ready(1)
    removal = removal_ref[...].astype(F32)
    norm = group_sums(removal * removal, ones) * (1.0 / GROUP_DIMENSION)
    kappa = removal * lax.rsqrt(norm + KEY_EPS) * GROUP_DIMENSION ** (-0.5)
    away = kappa * rate_ref[...].astype(F32) * inverse
    keys = key_ref[...].astype(F32) * inverse
    return log_step, cum, middle, past, kappa, away, keys


def range_kernel(
    owners, fade_hbm, key_hbm, value_hbm, removal_hbm, rate_hbm, *rest
):
    send_refs = rest[:owners]
    solved_ref, loaded, held, load_sems, sems = rest[owners:]
    sources = (fade_hbm, removal_hbm, rate_hbm, key_hbm, value_hbm)
    loads = [
        pltpu.make_async_copy(source, loaded.at[k], load_sems.at[k])
        for k, source in enumerate(sources)
    ]
    for load in loads:
        load.start()

    def ready(stage):
        for load in loads[:1] if stage == 0 else loads[1:]:
            load.wait()

    fade_ref, removal_ref, rate_ref, key_ref, value_ref = (
        loaded.at[k] for k in range(len(sources))
    )
    me = lax.axis_index("seq")
    tokens, width = fade_ref.shape
    pairs = width // PAIR
    per_owner = held.shape[1]
    d = GROUP_DIMENSION

    ones = group_ones()
    log_step, cum, middle, past, kappa, away, keys = key_side(
        fade_ref, removal_ref, rate_ref, key_ref, ones, ready
    )
    end = cum[tokens - 1 : tokens]
    to_end = jnp.exp(end - middle)
    gamma_end = jnp.exp(end)
    toward_mid = -kappa * jnp.exp(past - log_step)
    toward_abs = toward_mid * jnp.exp(middle)

    cuts = [slice(p * PAIR, (p + 1) * PAIR) for p in range(pairs)]
    block = iota((d, 2 * PAIR), 1) % PAIR
    is_low = block < d
    strict = iota((d, 2 * PAIR), 0) < block % d
    unit = iota((d, 2 * PAIR), 0) == block % d
    low = (iota((d, PAIR), 1) < d).astype(F32).astype(BF16)
    high = (iota((d, PAIR), 1) >= d).astype(F32).astype(BF16)

    lanes = iota((tokens, PAIR), 1)
    low_rows = (lanes < d).astype(F32).astype(BF16)
    high_rows = (lanes >= d).astype(F32).astype(BF16)
    late_rows = (iota((tokens, PAIR), 0) >= tokens // 2).astype(F32).astype(BF16)
    eye = (iota((PAIR, PAIR), 0) == iota((PAIR, PAIR), 1)).astype(F32).astype(BF16)
    known, values, inverses, across, powers = [], [], [], [], []
    scored = []
    for cut in cuts:
        query = toward_mid[:, cut].astype(BF16)
        own = low_rows, high_rows
        every = stack(*(query * mask for mask in own))
        recent = stack(*(query * late_rows * mask for mask in own))
        a_parts, k_parts = split(away[:, cut]), split(keys[:, cut])

        def against(part, queries):
            lefts = [stack(a[part], k[part]) for a, k in zip(a_parts, k_parts)]
            return mm_turned(side(*lefts), side(queries, queries))

        scored.append((against(slice(0, d), every), against(slice(d, 2 * d), recent)))
    turned = [
        mm_turned(eye, stack(toward_abs[:, cut].astype(BF16), value_ref[:, cut]))
        for cut in cuts
    ]
    mixes = []
    for early, later in scored:
        mix_early, mix_later = early[:d], later[:d]
        power = jnp.where(strict, jnp.where(is_low, mix_early, mix_later), 0.0)
        inverses.append(jnp.where(unit, 1.0, power))
        powers.append(power.astype(BF16))
        across.append(jnp.where(is_low, 0.0, mix_early))
        key_early = jnp.where(is_low & ~strict, 0.0, early[d:])
        key_later = jnp.where(~is_low & strict, later[d:], 0.0)
        mixes.append(stack(key_early.astype(BF16), key_later.astype(BF16)))
    none = jnp.zeros((tokens, tokens), BF16)
    for both, mixed in zip(turned, mixes):
        start, value_t = both[:, :tokens], both[:, tokens:].astype(BF16)
        mixed = stack(side(mixed[:, :tokens], none), side(none, mixed[:, tokens:]))
        moved = mm(side(value_t[:d], value_t[d:]), mixed)
        known.append(stack(side(start[:d], start[d:]), moved))
        values.append(value_t)

    reach = 1
    while reach < d:
        for p in range(pairs):
            factor = lane_blocks(powers[p], low, high)
            if reach == 1:
                powers[p] = mm(powers[p], factor).astype(BF16)
            elif reach * 2 < d:
                out = mm(stack(inverses[p].astype(BF16), powers[p]), factor)
                inverses[p] = inverses[p] + out[:d]
                powers[p] = out[d:].astype(BF16)
            else:
                inverses[p] = inverses[p] + mm(inverses[p].astype(BF16), factor)
        reach *= 2
    solved = []
    for p in range(pairs):
        rest = jnp.where(strict, inverses[p], 0.0).astype(BF16)
        factor = lane_blocks(rest, low, high)
        left = stack(known[p].astype(BF16), across[p].astype(BF16))
        out = mm(left, factor)
        solved.append(known[p] + out[:tokens])
        across[p] = (across[p] + out[tokens:]).astype(BF16)
    for p in range(pairs):
        one, two = across[p][:, :PAIR], across[p][:, PAIR:]
        none = jnp.zeros_like(one)
        factor = stack(side(one, none), side(none, none), side(none, two), side(none, none))
        solved[p] = (solved[p] + mm(solved[p].astype(BF16), factor)).astype(BF16)

    lane = iota((d, PAIR), 1)
    sub = iota((d, PAIR), 0)
    none = jnp.zeros((d, PAIR), BF16)
    for p, cut in enumerate(cuts):
        away_end = (away[:, cut] * to_end[:, cut]).astype(BF16)
        away_end = side(away_end, jnp.zeros_like(away_end))
        keys_end = side(*split(keys[:, cut] * to_end[:, cut]))
        lefts = [
            side(
                solved[p][:, i * tokens : (i + 1) * tokens],
                stack(none, values[p][i * d : (i + 1) * d]),
            )
            for i in range(2)
        ]
        ended = folded(stack(*lefts), stack(away_end, keys_end))
        for i in range(2):
            solved_ref[2 * p + i] = lefts[i]
            stay = jnp.where(lane == sub + i * d, gamma_end[:, cut], 0.0)
            state_map = ended[2 * i * d : (2 * i + 1) * d] + stay
            state_add = ended[(2 * i + 1) * d : (2 * i + 2) * d]
            if i == 0:
                state_add = pltpu.roll(state_add, d, 1)
            else:
                state_map = pltpu.roll(state_map, d, 1)
            head = 2 * p + i
            slot = lax.rem(head // per_owner - me % owners + owners, owners)
            held[slot, head % per_owner] = jnp.where(
                lane < d, state_map, state_add
            )

    copies = [
        pltpu.make_async_copy(held.at[k], send_refs[k], sems.at[k])
        for k in range(owners)
    ]
    for copy in copies:
        copy.start()
    for copy in copies:
        copy.wait()


def resident(count):
    return [pl.BlockSpec(memory_space=pltpu.VMEM)] * count


def limit(mib):
    return pltpu.CompilerParams(vmem_limit_bytes=mib << 20)


def range_pass(owners, fade, key, value, removal, rate):
    tokens, features = fade.shape
    heads = features // GROUP_DIMENSION
    block = (heads // owners, GROUP_DIMENSION, PAIR)
    out = pl.pallas_call(
        functools.partial(range_kernel, owners),
        in_specs=[pl.BlockSpec(memory_space=pltpu.HBM)] * 5,
        out_specs=[pl.BlockSpec(memory_space=pl.ANY)] * owners + resident(2),
        out_shape=[jax.ShapeDtypeStruct(block, F32)] * owners
        + [
            jax.ShapeDtypeStruct((heads, tokens, 2 * tokens), BF16),
            jax.ShapeDtypeStruct((5, tokens, features), BF16),
        ],
        scratch_shapes=[
            pltpu.VMEM((owners,) + block, F32),
            pltpu.SemaphoreType.DMA((5,)),
            pltpu.SemaphoreType.DMA((owners,)),
        ],
        compiler_params=limit(40),
        name="range_pass",
    )(fade, key, value, removal, rate)
    return out[:owners], out[owners:]


def read_kernel(
    reader_ref,
    extra_ref,
    solved_ref,
    loaded,
    lift_high_ref,
    lift_low_ref,
    within_ref,
    bonus_ref,
):
    fade_ref, removal_ref, rate_ref, key_ref, value_ref = (
        loaded.at[k] for k in range(loaded.shape[0])
    )
    tokens, width = fade_ref.shape
    d = GROUP_DIMENSION
    ones = group_ones()
    late = late_columns(tokens)
    seen = iota((tokens, tokens), 0) <= iota((tokens, tokens), 1)
    _, cum, middle, past, _, away, keys = key_side(
        fade_ref, removal_ref, rate_ref, key_ref, ones
    )
    reader = reader_ref[...].astype(F32)
    value = value_ref[...].astype(F32)
    bonus = group_sums(reader * key_ref[...].astype(F32) * extra_ref[...], ones)
    bonus_ref[...] = bonus * value
    reader_mid = reader * jnp.exp(past)
    reader_abs = reader_mid * jnp.exp(middle)

    for p in range(width // PAIR):
        cut = slice(p * PAIR, (p + 1) * PAIR)
        early, later = scores(
            late,
            split(away[:, cut]),
            split(keys[:, cut]),
            split(reader_mid[:, cut].T),
            3,
        )
        start = reader_abs[:, cut].T
        for i in range(2):
            lanes = slice(i * tokens, (i + 1) * tokens)
            rows = slice(i * d, (i + 1) * d)
            at = slice(p * PAIR + i * d, p * PAIR + (i + 1) * d)

            def read(part):
                whole = stack(early[part, lanes], later[part, lanes])
                return side(*split(jnp.where(seen, whole, 0.0)))

            out = folded(
                solved_ref[2 * p + i], stack(read(slice(0, d)), read(slice(d, 2 * d)))
            )
            within_ref[at] = out[d:]
            lift_high_ref[at], lift_low_ref[at] = split(start[rows] + out[:d])


def read_pass(reader, extra, solved, loaded):
    tokens, features = reader.shape
    return pl.pallas_call(
        read_kernel,
        in_specs=resident(4),
        out_specs=resident(4),
        out_shape=[
            jax.ShapeDtypeStruct((features, tokens), BF16),
            jax.ShapeDtypeStruct((features, tokens), BF16),
            jax.ShapeDtypeStruct((features, tokens), F32),
            jax.ShapeDtypeStruct((tokens, features), F32),
        ],
        compiler_params=limit(40),
        name="read_pass",
    )(reader, extra, solved, loaded)


def chain_kernel(owners, *refs):
    got_refs = refs[:owners]
    state_refs = refs[owners : 2 * owners]
    final_ref, ranges, states = refs[2 * owners :]
    me = lax.axis_index("seq")
    per_owner = got_refs[0].shape[0]
    for k in range(owners):
        ranges[lax.rem(me - k + owners, owners)] = got_refs[k][...]
    d = GROUP_DIMENSION
    lane = iota((d // 2, PAIR), 1)
    none = jnp.zeros((d, 2 * PAIR), BF16)
    current = []
    for q in range(per_owner):
        states[0, q] = jnp.zeros((d // 2, PAIR), F32)
        current.append(ranges[0, q])
    for i in range(1, owners):
        for q in range(per_owner):
            now = current[q]
            states[i, q] = jnp.where(
                lane < d, pltpu.roll(now[: d // 2], d, 1), now[d // 2 :]
            )
            both = ranges[i, q]
            maps = side(*split(pltpu.roll(both, d, 1)))
            out = mm(stack(*split(now)), stack(none, maps))
            current[q] = out[:d, :PAIR] + out[:d, PAIR:] + out[d:, :PAIR] + both
    for q in range(per_owner):
        final_ref[q * d : (q + 1) * d, :] = pltpu.roll(current[q], d, 1)[:, :d]
    for k in range(owners):
        state_refs[k][...] = states[lax.rem(me + k, owners)]


def chain(got):
    owners = len(got)
    per_owner = got[0].shape[0]
    block = (per_owner, GROUP_DIMENSION // 2, PAIR)
    rows = per_owner * GROUP_DIMENSION
    out = pl.pallas_call(
        functools.partial(chain_kernel, owners),
        in_specs=resident(owners),
        out_specs=resident(owners + 1),
        out_shape=[jax.ShapeDtypeStruct(block, F32)] * owners
        + [jax.ShapeDtypeStruct((rows, GROUP_DIMENSION), F32)],
        scratch_shapes=[
            pltpu.VMEM((owners,) + got[0].shape, F32),
            pltpu.VMEM((owners,) + block, F32),
        ],
        compiler_params=limit(40),
        name="chain",
    )(*got)
    return out[:owners], out[owners]


def finish_kernel(owners, *refs):
    state_refs = refs[:owners]
    lift_high_ref, lift_low_ref, within_ref, bonus_ref, gain_ref = refs[
        owners : owners + 5
    ]
    out_ref, states = refs[owners + 5 :]
    me = lax.axis_index("seq")
    per_owner = state_refs[0].shape[0]
    width = out_ref.shape[1]
    d = GROUP_DIMENSION

    for k in range(owners):
        states[lax.rem(me % owners - k + owners, owners)] = state_refs[k][...]

    lane = iota((d // 2, PAIR), 1)
    for p in range(width // PAIR):
        normed = []
        for i in range(2):
            head = 2 * p + i
            packed = states[head // per_owner, head % per_owner]
            state = split(
                stack(
                    jnp.where(lane < d, packed, 0.0),
                    jnp.where(lane >= d, packed, 0.0),
                )
            )
            at = slice(p * PAIR + i * d, p * PAIR + (i + 1) * d)
            high, low = lift_high_ref[at], lift_low_ref[at]
            result = within_ref[at] + mm3(
                state, (stack(high, high), stack(low, low))
            )
            average = jnp.mean(result, axis=0, keepdims=True)
            centered = result - average
            spread = jnp.mean(centered * centered, axis=0, keepdims=True)
            normed.append(centered * lax.rsqrt(spread + NORM_EPS))
        cut = slice(p * PAIR, (p + 1) * PAIR)
        turned = stack(*normed).T
        out_ref[:, cut] = (turned * gain_ref[:, cut] + bonus_ref[:, cut]).astype(BF16)


def finish(states, lift_high, lift_low, within, bonus, gain):
    owners = len(states)
    tokens, features = bonus.shape
    return pl.pallas_call(
        functools.partial(finish_kernel, owners),
        in_specs=resident(owners + 5),
        out_specs=resident(1)[0],
        out_shape=jax.ShapeDtypeStruct((tokens, features), BF16),
        scratch_shapes=[pltpu.VMEM((owners,) + states[0].shape, F32)],
        compiler_params=limit(40),
        name="finish",
    )(*states, lift_high, lift_low, within, bonus, gain)


def shifted(value, by, members):
    return lax.ppermute(value, "seq", [(i, (i + by) % members) for i in range(members)])


def relay_states(both, members):
    d = GROUP_DIMENSION
    local_map, local_add = both[:, :, :d], both[:, :, d:]

    def relay(_, carried):
        pairs = [(i, i + 1) for i in range(members - 1)]
        incoming = lax.ppermute(carried[1], "seq", pairs)
        moved = jnp.einsum(
            "hvk,hkj->hvj", incoming, local_map, precision=lax.Precision.HIGHEST
        )
        return (incoming, moved + local_add)

    first = (jnp.zeros_like(local_add), local_add)
    incoming, leaving = lax.fori_loop(0, members - 1, relay, first)
    here = lax.axis_index("seq")
    closing = lax.psum(jnp.where(here == members - 1, leaving, 0.0), "seq")
    closing = closing.reshape(-1, d)
    rows = closing.shape[0] // members
    final = lax.dynamic_slice_in_dim(closing, here * rows, rows, 0)
    packed = jnp.concatenate([incoming[:, : d // 2], incoming[:, d // 2 :]], axis=2)
    return packed, final


def on_device(reader, fade, key, value, removal, rate, extra, gain):
    members = lax.axis_size("seq")
    features = reader.shape[2]
    heads = features // GROUP_DIMENSION
    owners = members if heads % members == 0 else 1
    keyed = (fade[0], key[0], value[0], removal[0], rate[0])
    keyed = [pltpu.with_memory_space_constraint(x, pltpu.HBM) for x in keyed]
    sends, kept = range_pass(owners, *keyed)
    parts = read_pass(reader[0], extra.reshape(1, features), *kept)
    if owners > 1:
        got = [sends[0]] + [shifted(sends[k], k, members) for k in range(1, owners)]
        got, parts = lax.optimization_barrier((got, parts))
        states, final = chain(got)
        states = [states[0]] + [
            shifted(states[k], k, members) for k in range(1, owners)
        ]
    else:
        packed, final = relay_states(sends[0], members)
        states = [packed]
    blended = finish(states, *parts, gain.reshape(1, features))
    return (blended[None], final[None])


def solution(mesh):
    tokens = P(("groups", "dp"), "seq", None)
    return jax.shard_map(
        on_device,
        mesh=mesh,
        in_specs=(tokens,) * 6 + (P(), P()),
        out_specs=(tokens, tokens),
        check_vma=False,
    )
```

```python
import functools

import jax
import jax.numpy as jnp
from jax import lax
from jax.experimental import pallas as pl
from jax.experimental.pallas import tpu as pltpu
from jax.sharding import PartitionSpec as P

GROUP_DIMENSION = 64
PAIR = 2 * GROUP_DIMENSION
KEY_EPS = 1e-05
NORM_EPS = 0.00064

F32 = jnp.float32
BF16 = jnp.bfloat16


def mm(left, right):
    return jnp.dot(left, right, preferred_element_type=F32)


def mm_turned(left, right):
    return lax.dot_general(
        left, right, (((1,), (1,)), ((), ())), preferred_element_type=F32
    )


def split(x):
    high = x.astype(BF16)
    return high, (x - high.astype(F32)).astype(BF16)


def side(*parts):
    return jnp.concatenate(parts, axis=1)


def stack(*parts):
    return jnp.concatenate(parts, axis=0)


def mm3(left, right):
    lh, ll = left
    rh, rl = right
    return mm(side(lh, ll), stack(rh, rh)) + mm(lh, rl)


def iota(shape, axis):
    return lax.broadcasted_iota(jnp.int32, shape, axis)


def group_ones():
    same = (iota((PAIR, PAIR), 0) // GROUP_DIMENSION) == (
        iota((PAIR, PAIR), 1) // GROUP_DIMENSION
    )
    ones = same.astype(F32).astype(BF16)
    return stack(ones, ones)


def group_sums(x, ones):
    parts = []
    for p in range(x.shape[1] // PAIR):
        high, low = split(x[:, p * PAIR : (p + 1) * PAIR])
        parts.append(mm(side(high, low), ones))
    return side(*parts)


def block_diagonal(x):
    top, bottom = x[:GROUP_DIMENSION], x[GROUP_DIMENSION:]
    none = jnp.zeros_like(top)
    return stack(side(top, none), side(none, bottom))


def folded(left, right):
    full = mm(left, right)
    return full[:, :PAIR] + full[:, PAIR:]


def lane_blocks(x, low, high):
    return stack(x * low, x * high)


def scores(late, away, keys, query, terms):
    half = away[0].shape[0] // 2
    qh, ql = (block_diagonal(q) for q in query)

    def against(part, high, low):
        left = [stack(a[part], k[part]) for a, k in zip(away, keys)]
        out = mm(side(*left), stack(high, high))
        return out + mm(left[0], low) if terms == 3 else out

    early = against(slice(0, half), qh, ql)
    later = against(slice(half, 2 * half), qh * late, ql * late)
    return early, later


def late_columns(tokens):
    lane = iota((PAIR, 2 * tokens), 1) % tokens
    return (lane >= tokens // 2).astype(F32).astype(BF16)


def cumulative(log_step):
    tokens = log_step.shape[0]
    shape = (tokens, tokens)
    lower = (iota(shape, 0) >= iota(shape, 1)).astype(F32).astype(BF16)
    return mm(side(lower, lower), stack(*split(log_step)))


def key_side(fade_ref, removal_ref, rate_ref, key_ref, ones, ready=lambda k: None):
    half = fade_ref.shape[0] // 2
    ready(0)
    log_step = -jnp.exp(fade_ref[...].astype(F32))
    cum = cumulative(log_step)
    middle = cum[half - 1 : half]
    past = cum - middle
    inverse = jnp.exp(-past)
    ready(1)
    removal = removal_ref[...].astype(F32)
    norm = group_sums(removal * removal, ones) * (1.0 / GROUP_DIMENSION)
    kappa = removal * lax.rsqrt(norm + KEY_EPS) * GROUP_DIMENSION ** (-0.5)
    away = kappa * rate_ref[...].astype(F32) * inverse
    keys = key_ref[...].astype(F32) * inverse
    return log_step, cum, middle, past, kappa, away, keys


def range_kernel(
    owners, fade_hbm, key_hbm, value_hbm, removal_hbm, rate_hbm, *rest
):
    send_refs = rest[:owners]
    solved_ref, loaded, held, load_sems, sems = rest[owners:]
    sources = (fade_hbm, removal_hbm, rate_hbm, key_hbm, value_hbm)
    loads = [
        pltpu.make_async_copy(source, loaded.at[k], load_sems.at[k])
        for k, source in enumerate(sources)
    ]
    for load in loads:
        load.start()

    def ready(stage):
        for load in loads[:1] if stage == 0 else loads[1:]:
            load.wait()

    fade_ref, removal_ref, rate_ref, key_ref, value_ref = (
        loaded.at[k] for k in range(len(sources))
    )
    me = lax.axis_index("seq")
    tokens, width = fade_ref.shape
    pairs = width // PAIR
    per_owner = held.shape[1]
    d = GROUP_DIMENSION

    ones = group_ones()
    log_step, cum, middle, past, kappa, away, keys = key_side(
        fade_ref, removal_ref, rate_ref, key_ref, ones, ready
    )
    end = cum[tokens - 1 : tokens]
    to_end = jnp.exp(end - middle)
    gamma_end = jnp.exp(end)
    toward_mid = -kappa * jnp.exp(past - log_step)
    toward_abs = toward_mid * jnp.exp(middle)

    cuts = [slice(p * PAIR, (p + 1) * PAIR) for p in range(pairs)]
    block = iota((d, PAIR), 1)
    is_low = block < d
    strict = iota((d, PAIR), 0) < block % d
    unit = iota((d, PAIR), 0) == block % d
    low = (iota((d, PAIR), 1) < d).astype(F32).astype(BF16)
    high = (iota((d, PAIR), 1) >= d).astype(F32).astype(BF16)

    lanes = iota((tokens, PAIR), 1)
    low_rows = (lanes < d).astype(F32).astype(BF16)
    high_rows = (lanes >= d).astype(F32).astype(BF16)
    late_rows = (iota((tokens, PAIR), 0) >= tokens // 2).astype(F32).astype(BF16)
    eye = (iota((PAIR, PAIR), 0) == iota((PAIR, PAIR), 1)).astype(F32).astype(BF16)
    known, values, inverses, across, powers = [], [], [], [], []
    scored = []
    for cut in cuts:
        query = toward_mid[:, cut].astype(BF16)
        own = low_rows, high_rows
        every = stack(*(query * mask for mask in own))
        recent = stack(*(query * late_rows * mask for mask in own))
        a_parts, k_parts = split(away[:, cut]), split(keys[:, cut])

        def against(part, queries):
            lefts = [stack(a[part], k[part]) for a, k in zip(a_parts, k_parts)]
            return mm_turned(side(*lefts), side(queries, queries))

        scored.append((against(slice(0, d), every), against(slice(d, 2 * d), recent)))
    turned = [
        mm_turned(eye, stack(toward_abs[:, cut].astype(BF16), value_ref[:, cut]))
        for cut in cuts
    ]
    mixes = []
    for early, later in scored:
        for i in range(2):
            mine = slice(i * tokens, (i + 1) * tokens)
            one, two = early[:, mine], later[:, mine]
            power = jnp.where(strict, jnp.where(is_low, one[:d], two[:d]), 0.0)
            inverses.append(jnp.where(unit, 1.0, power))
            powers.append(power.astype(BF16))
            across.append(jnp.where(is_low, 0.0, one[:d]))
            key_early = jnp.where(is_low & ~strict, 0.0, one[d:])
            key_later = jnp.where(~is_low & strict, two[d:], 0.0)
            mixes.append(stack(key_early.astype(BF16), key_later.astype(BF16)))
    for both in turned:
        for i in range(2):
            mine = slice(i * d, (i + 1) * d)
            value_h = both[mine, tokens:].astype(BF16)
            moved = mm(value_h, mixes[len(known)])
            known.append(stack(both[mine, :tokens], moved))
            values.append(value_h)

    count = 2 * pairs
    reach = 1
    while reach < d:
        for h in range(count):
            factor = lane_blocks(powers[h], low, high)
            if reach == 1:
                powers[h] = mm(powers[h], factor).astype(BF16)
            elif reach * 2 < d:
                out = mm(stack(inverses[h].astype(BF16), powers[h]), factor)
                inverses[h] = inverses[h] + out[:d]
                powers[h] = out[d:].astype(BF16)
            else:
                inverses[h] = inverses[h] + mm(inverses[h].astype(BF16), factor)
        reach *= 2
    for h in range(count):
        rest = jnp.where(strict, inverses[h], 0.0).astype(BF16)
        left = stack(known[h].astype(BF16), across[h].astype(BF16))
        out = mm(left, lane_blocks(rest, low, high))
        known[h] = known[h] + out[:tokens]
        across[h] = (across[h] + out[tokens:]).astype(BF16)
    solved = []
    for h in range(count):
        factor = stack(across[h], jnp.zeros_like(across[h]))
        solved.append((known[h] + mm(known[h].astype(BF16), factor)).astype(BF16))

    lane = iota((d, PAIR), 1)
    sub = iota((d, PAIR), 0)
    none = jnp.zeros((d, PAIR), BF16)
    for p, cut in enumerate(cuts):
        away_end = (away[:, cut] * to_end[:, cut]).astype(BF16)
        away_end = side(away_end, jnp.zeros_like(away_end))
        keys_end = side(*split(keys[:, cut] * to_end[:, cut]))
        lefts = [
            side(solved[2 * p + i], stack(none, values[2 * p + i]))
            for i in range(2)
        ]
        ended = folded(stack(*lefts), stack(away_end, keys_end))
        for i in range(2):
            solved_ref[2 * p + i] = lefts[i]
            stay = jnp.where(lane == sub + i * d, gamma_end[:, cut], 0.0)
            state_map = ended[2 * i * d : (2 * i + 1) * d] + stay
            state_add = ended[(2 * i + 1) * d : (2 * i + 2) * d]
            if i == 0:
                state_add = pltpu.roll(state_add, d, 1)
            else:
                state_map = pltpu.roll(state_map, d, 1)
            head = 2 * p + i
            slot = lax.rem(head // per_owner - me % owners + owners, owners)
            held[slot, head % per_owner] = jnp.where(
                lane < d, state_map, state_add
            )

    copies = [
        pltpu.make_async_copy(held.at[k], send_refs[k], sems.at[k])
        for k in range(owners)
    ]
    for copy in copies:
        copy.start()
    for copy in copies:
        copy.wait()


def resident(count):
    return [pl.BlockSpec(memory_space=pltpu.VMEM)] * count


def limit(mib):
    return pltpu.CompilerParams(vmem_limit_bytes=mib << 20)


def range_pass(owners, fade, key, value, removal, rate):
    tokens, features = fade.shape
    heads = features // GROUP_DIMENSION
    block = (heads // owners, GROUP_DIMENSION, PAIR)
    out = pl.pallas_call(
        functools.partial(range_kernel, owners),
        in_specs=[pl.BlockSpec(memory_space=pltpu.HBM)] * 5,
        out_specs=[pl.BlockSpec(memory_space=pl.ANY)] * owners + resident(2),
        out_shape=[jax.ShapeDtypeStruct(block, F32)] * owners
        + [
            jax.ShapeDtypeStruct((heads, tokens, 2 * tokens), BF16),
            jax.ShapeDtypeStruct((5, tokens, features), BF16),
        ],
        scratch_shapes=[
            pltpu.VMEM((owners,) + block, F32),
            pltpu.SemaphoreType.DMA((5,)),
            pltpu.SemaphoreType.DMA((owners,)),
        ],
        compiler_params=limit(40),
        name="range_pass",
    )(fade, key, value, removal, rate)
    return out[:owners], out[owners:]


def read_kernel(
    reader_ref,
    extra_ref,
    solved_ref,
    loaded,
    lift_high_ref,
    lift_low_ref,
    within_ref,
    bonus_ref,
):
    fade_ref, removal_ref, rate_ref, key_ref, value_ref = (
        loaded.at[k] for k in range(loaded.shape[0])
    )
    tokens, width = fade_ref.shape
    d = GROUP_DIMENSION
    ones = group_ones()
    late = late_columns(tokens)
    seen = iota((tokens, tokens), 0) <= iota((tokens, tokens), 1)
    _, cum, middle, past, _, away, keys = key_side(
        fade_ref, removal_ref, rate_ref, key_ref, ones
    )
    reader = reader_ref[...].astype(F32)
    value = value_ref[...].astype(F32)
    bonus = group_sums(reader * key_ref[...].astype(F32) * extra_ref[...], ones)
    bonus_ref[...] = bonus * value
    reader_mid = reader * jnp.exp(past)
    reader_abs = reader_mid * jnp.exp(middle)

    for p in range(width // PAIR):
        cut = slice(p * PAIR, (p + 1) * PAIR)
        early, later = scores(
            late,
            split(away[:, cut]),
            split(keys[:, cut]),
            split(reader_mid[:, cut].T),
            3,
        )
        start = reader_abs[:, cut].T
        for i in range(2):
            lanes = slice(i * tokens, (i + 1) * tokens)
            rows = slice(i * d, (i + 1) * d)
            at = slice(p * PAIR + i * d, p * PAIR + (i + 1) * d)

            def read(part):
                whole = stack(early[part, lanes], later[part, lanes])
                return side(*split(jnp.where(seen, whole, 0.0)))

            out = folded(
                solved_ref[2 * p + i], stack(read(slice(0, d)), read(slice(d, 2 * d)))
            )
            within_ref[at] = out[d:]
            lift_high_ref[at], lift_low_ref[at] = split(start[rows] + out[:d])


def read_pass(reader, extra, solved, loaded):
    tokens, features = reader.shape
    return pl.pallas_call(
        read_kernel,
        in_specs=resident(4),
        out_specs=resident(4),
        out_shape=[
            jax.ShapeDtypeStruct((features, tokens), BF16),
            jax.ShapeDtypeStruct((features, tokens), BF16),
            jax.ShapeDtypeStruct((features, tokens), F32),
            jax.ShapeDtypeStruct((tokens, features), F32),
        ],
        compiler_params=limit(40),
        name="read_pass",
    )(reader, extra, solved, loaded)


def chain_kernel(owners, *refs):
    got_refs = refs[:owners]
    state_refs = refs[owners : 2 * owners]
    final_ref, ranges, states = refs[2 * owners :]
    me = lax.axis_index("seq")
    per_owner = got_refs[0].shape[0]
    for k in range(owners):
        ranges[lax.rem(me - k + owners, owners)] = got_refs[k][...]
    d = GROUP_DIMENSION
    lane = iota((d // 2, PAIR), 1)
    none = jnp.zeros((d, 2 * PAIR), BF16)
    current = []
    for q in range(per_owner):
        states[0, q] = jnp.zeros((d // 2, PAIR), F32)
        current.append(ranges[0, q])
    for i in range(1, owners):
        for q in range(per_owner):
            now = current[q]
            states[i, q] = jnp.where(
                lane < d, pltpu.roll(now[: d // 2], d, 1), now[d // 2 :]
            )
            both = ranges[i, q]
            maps = side(*split(pltpu.roll(both, d, 1)))
            out = mm(stack(*split(now)), stack(none, maps))
            current[q] = out[:d, :PAIR] + out[:d, PAIR:] + out[d:, :PAIR] + both
    for q in range(per_owner):
        final_ref[q * d : (q + 1) * d, :] = pltpu.roll(current[q], d, 1)[:, :d]
    for k in range(owners):
        state_refs[k][...] = states[lax.rem(me + k, owners)]


def chain(got):
    owners = len(got)
    per_owner = got[0].shape[0]
    block = (per_owner, GROUP_DIMENSION // 2, PAIR)
    rows = per_owner * GROUP_DIMENSION
    out = pl.pallas_call(
        functools.partial(chain_kernel, owners),
        in_specs=resident(owners),
        out_specs=resident(owners + 1),
        out_shape=[jax.ShapeDtypeStruct(block, F32)] * owners
        + [jax.ShapeDtypeStruct((rows, GROUP_DIMENSION), F32)],
        scratch_shapes=[
            pltpu.VMEM((owners,) + got[0].shape, F32),
            pltpu.VMEM((owners,) + block, F32),
        ],
        compiler_params=limit(40),
        name="chain",
    )(*got)
    return out[:owners], out[owners]


def finish_kernel(owners, *refs):
    state_refs = refs[:owners]
    lift_high_ref, lift_low_ref, within_ref, bonus_ref, gain_ref = refs[
        owners : owners + 5
    ]
    out_ref, states = refs[owners + 5 :]
    me = lax.axis_index("seq")
    per_owner = state_refs[0].shape[0]
    width = out_ref.shape[1]
    d = GROUP_DIMENSION

    for k in range(owners):
        states[lax.rem(me % owners - k + owners, owners)] = state_refs[k][...]

    lane = iota((d // 2, PAIR), 1)
    for p in range(width // PAIR):
        normed = []
        for i in range(2):
            head = 2 * p + i
            packed = states[head // per_owner, head % per_owner]
            state = split(
                stack(
                    jnp.where(lane < d, packed, 0.0),
                    jnp.where(lane >= d, packed, 0.0),
                )
            )
            at = slice(p * PAIR + i * d, p * PAIR + (i + 1) * d)
            high, low = lift_high_ref[at], lift_low_ref[at]
            result = within_ref[at] + mm3(
                state, (stack(high, high), stack(low, low))
            )
            average = jnp.mean(result, axis=0, keepdims=True)
            centered = result - average
            spread = jnp.mean(centered * centered, axis=0, keepdims=True)
            normed.append(centered * lax.rsqrt(spread + NORM_EPS))
        cut = slice(p * PAIR, (p + 1) * PAIR)
        turned = stack(*normed).T
        out_ref[:, cut] = (turned * gain_ref[:, cut] + bonus_ref[:, cut]).astype(BF16)


def finish(states, lift_high, lift_low, within, bonus, gain):
    owners = len(states)
    tokens, features = bonus.shape
    return pl.pallas_call(
        functools.partial(finish_kernel, owners),
        in_specs=resident(owners + 5),
        out_specs=resident(1)[0],
        out_shape=jax.ShapeDtypeStruct((tokens, features), BF16),
        scratch_shapes=[pltpu.VMEM((owners,) + states[0].shape, F32)],
        compiler_params=limit(40),
        name="finish",
    )(*states, lift_high, lift_low, within, bonus, gain)


def shifted(value, by, members):
    return lax.ppermute(value, "seq", [(i, (i + by) % members) for i in range(members)])


def relay_states(both, members):
    d = GROUP_DIMENSION
    local_map, local_add = both[:, :, :d], both[:, :, d:]

    def relay(_, carried):
        pairs = [(i, i + 1) for i in range(members - 1)]
        incoming = lax.ppermute(carried[1], "seq", pairs)
        moved = jnp.einsum(
            "hvk,hkj->hvj", incoming, local_map, precision=lax.Precision.HIGHEST
        )
        return (incoming, moved + local_add)

    first = (jnp.zeros_like(local_add), local_add)
    incoming, leaving = lax.fori_loop(0, members - 1, relay, first)
    here = lax.axis_index("seq")
    closing = lax.psum(jnp.where(here == members - 1, leaving, 0.0), "seq")
    closing = closing.reshape(-1, d)
    rows = closing.shape[0] // members
    final = lax.dynamic_slice_in_dim(closing, here * rows, rows, 0)
    packed = jnp.concatenate([incoming[:, : d // 2], incoming[:, d // 2 :]], axis=2)
    return packed, final


def on_device(reader, fade, key, value, removal, rate, extra, gain):
    members = lax.axis_size("seq")
    features = reader.shape[2]
    heads = features // GROUP_DIMENSION
    owners = members if heads % members == 0 else 1
    keyed = (fade[0], key[0], value[0], removal[0], rate[0])
    keyed = [pltpu.with_memory_space_constraint(x, pltpu.HBM) for x in keyed]
    sends, kept = range_pass(owners, *keyed)
    parts = read_pass(reader[0], extra.reshape(1, features), *kept)
    if owners > 1:
        got = [sends[0]] + [shifted(sends[k], k, members) for k in range(1, owners)]
        got, parts = lax.optimization_barrier((got, parts))
        states, final = chain(got)
        states = [states[0]] + [
            shifted(states[k], k, members) for k in range(1, owners)
        ]
    else:
        packed, final = relay_states(sends[0], members)
        states = [packed]
    blended = finish(states, *parts, gain.reshape(1, features))
    return (blended[None], final[None])


def solution(mesh):
    tokens = P(("groups", "dp"), "seq", None)
    return jax.shard_map(
        on_device,
        mesh=mesh,
        in_specs=(tokens,) * 6 + (P(), P()),
        out_specs=(tokens, tokens),
        check_vma=False,
    )
```

```python
import functools

import jax
import jax.numpy as jnp
from jax import lax
from jax.experimental import pallas as pl
from jax.experimental.pallas import tpu as pltpu
from jax.sharding import PartitionSpec as P

GROUP_DIMENSION = 64
PAIR = 2 * GROUP_DIMENSION
KEY_EPS = 1e-05
NORM_EPS = 0.00064

F32 = jnp.float32
BF16 = jnp.bfloat16


def mm(left, right):
    return jnp.dot(left, right, preferred_element_type=F32)


def mm_turned(left, right):
    return lax.dot_general(
        left, right, (((1,), (1,)), ((), ())), preferred_element_type=F32
    )


def split(x):
    high = x.astype(BF16)
    return high, (x - high.astype(F32)).astype(BF16)


def side(*parts):
    return jnp.concatenate(parts, axis=1)


def stack(*parts):
    return jnp.concatenate(parts, axis=0)


def mm3(left, right):
    lh, ll = left
    rh, rl = right
    return mm(side(lh, ll), stack(rh, rh)) + mm(lh, rl)


def iota(shape, axis):
    return lax.broadcasted_iota(jnp.int32, shape, axis)


def group_ones():
    same = (iota((PAIR, PAIR), 0) // GROUP_DIMENSION) == (
        iota((PAIR, PAIR), 1) // GROUP_DIMENSION
    )
    ones = same.astype(F32).astype(BF16)
    return stack(ones, ones)


def group_sums(x, ones):
    parts = []
    for p in range(x.shape[1] // PAIR):
        high, low = split(x[:, p * PAIR : (p + 1) * PAIR])
        parts.append(mm(side(high, low), ones))
    return side(*parts)


def block_diagonal(x):
    top, bottom = x[:GROUP_DIMENSION], x[GROUP_DIMENSION:]
    none = jnp.zeros_like(top)
    return stack(side(top, none), side(none, bottom))


def folded(left, right):
    full = mm(left, right)
    return full[:, :PAIR] + full[:, PAIR:]


def lane_blocks(x, low, high):
    return stack(x * low, x * high)


def scores(late, away, keys, query, terms):
    half = away[0].shape[0] // 2
    qh, ql = (block_diagonal(q) for q in query)

    def against(part, high, low):
        left = [stack(a[part], k[part]) for a, k in zip(away, keys)]
        out = mm(side(*left), stack(high, high))
        return out + mm(left[0], low) if terms == 3 else out

    early = against(slice(0, half), qh, ql)
    later = against(slice(half, 2 * half), qh * late, ql * late)
    return early, later


def late_columns(tokens):
    lane = iota((PAIR, 2 * tokens), 1) % tokens
    return (lane >= tokens // 2).astype(F32).astype(BF16)


def cumulative(log_step):
    tokens = log_step.shape[0]
    shape = (tokens, tokens)
    lower = (iota(shape, 0) >= iota(shape, 1)).astype(F32).astype(BF16)
    return mm(side(lower, lower), stack(*split(log_step)))


def key_side(fade_ref, removal_ref, rate_ref, key_ref, ones, ready=lambda k: None):
    half = fade_ref.shape[0] // 2
    ready(0)
    log_step = -jnp.exp(fade_ref[...].astype(F32))
    cum = cumulative(log_step)
    middle = cum[half - 1 : half]
    past = cum - middle
    inverse = jnp.exp(-past)
    ready(1)
    removal = removal_ref[...].astype(F32)
    norm = group_sums(removal * removal, ones) * (1.0 / GROUP_DIMENSION)
    kappa = removal * lax.rsqrt(norm + KEY_EPS) * GROUP_DIMENSION ** (-0.5)
    away = kappa * rate_ref[...].astype(F32) * inverse
    keys = key_ref[...].astype(F32) * inverse
    return log_step, cum, middle, past, kappa, away, keys


def range_kernel(
    owners, fade_hbm, key_hbm, value_hbm, removal_hbm, rate_hbm, *rest
):
    send_refs = rest[:owners]
    solved_ref, loaded, held, load_sems, sems = rest[owners:]
    sources = (fade_hbm, removal_hbm, rate_hbm, key_hbm, value_hbm)
    loads = [
        pltpu.make_async_copy(source, loaded.at[k], load_sems.at[k])
        for k, source in enumerate(sources)
    ]
    for load in loads:
        load.start()

    def ready(stage):
        for load in loads[:1] if stage == 0 else loads[1:]:
            load.wait()

    fade_ref, removal_ref, rate_ref, key_ref, value_ref = (
        loaded.at[k] for k in range(len(sources))
    )
    me = lax.axis_index("seq")
    tokens, width = fade_ref.shape
    pairs = width // PAIR
    per_owner = held.shape[1]
    d = GROUP_DIMENSION

    ones = group_ones()
    log_step, cum, middle, past, kappa, away, keys = key_side(
        fade_ref, removal_ref, rate_ref, key_ref, ones, ready
    )
    end = cum[tokens - 1 : tokens]
    to_end = jnp.exp(end - middle)
    gamma_end = jnp.exp(end)
    toward_mid = -kappa * jnp.exp(past - log_step)
    toward_abs = toward_mid * jnp.exp(middle)

    cuts = [slice(p * PAIR, (p + 1) * PAIR) for p in range(pairs)]
    block = iota((d, PAIR), 1)
    is_low = block < d
    strict = iota((d, PAIR), 0) < block % d
    unit = iota((d, PAIR), 0) == block % d
    low = (iota((d, PAIR), 1) < d).astype(F32).astype(BF16)
    high = (iota((d, PAIR), 1) >= d).astype(F32).astype(BF16)

    lanes = iota((tokens, PAIR), 1)
    low_rows = (lanes < d).astype(F32).astype(BF16)
    high_rows = (lanes >= d).astype(F32).astype(BF16)
    late_rows = (iota((tokens, PAIR), 0) >= tokens // 2).astype(F32).astype(BF16)
    eye = (iota((PAIR, PAIR), 0) == iota((PAIR, PAIR), 1)).astype(F32).astype(BF16)
    known, values, inverses, across, powers = [], [], [], [], []
    scored = []
    for cut in cuts:
        query = toward_mid[:, cut].astype(BF16)
        own = low_rows, high_rows
        every = stack(*(query * mask for mask in own))
        recent = stack(*(query * late_rows * mask for mask in own))
        a_parts, k_parts = split(away[:, cut]), split(keys[:, cut])

        def against(part, queries):
            lefts = [stack(a[part], k[part]) for a, k in zip(a_parts, k_parts)]
            return mm_turned(side(*lefts), side(queries, queries))

        scored.append((against(slice(0, d), every), against(slice(d, 2 * d), recent)))
    turned = [
        mm_turned(eye, stack(toward_abs[:, cut].astype(BF16), value_ref[:, cut]))
        for cut in cuts
    ]
    mixes = []
    for early, later in scored:
        for i in range(2):
            mine = slice(i * tokens, (i + 1) * tokens)
            one, two = early[:, mine], later[:, mine]
            power = jnp.where(strict, jnp.where(is_low, one[:d], two[:d]), 0.0)
            inverses.append(jnp.where(unit, 1.0, power))
            powers.append(power.astype(BF16))
            across.append(jnp.where(is_low, 0.0, one[:d]))
            key_early = jnp.where(is_low & ~strict, 0.0, one[d:])
            key_later = jnp.where(~is_low & strict, two[d:], 0.0)
            mixes.append(stack(key_early.astype(BF16), key_later.astype(BF16)))
    for both in turned:
        for i in range(2):
            mine = slice(i * d, (i + 1) * d)
            value_h = both[mine, tokens:].astype(BF16)
            moved = mm(value_h, mixes[len(known)])
            known.append(stack(both[mine, :tokens], moved))
            values.append(value_h)

    count = 2 * pairs
    reach = 1
    while reach < d:
        for h in range(count):
            factor = lane_blocks(powers[h], low, high)
            if reach == 1:
                powers[h] = mm(powers[h], factor).astype(BF16)
            elif reach * 2 < d:
                out = mm(stack(inverses[h].astype(BF16), powers[h]), factor)
                inverses[h] = inverses[h] + out[:d]
                powers[h] = out[d:].astype(BF16)
            else:
                inverses[h] = inverses[h] + mm(inverses[h].astype(BF16), factor)
        reach *= 2
    for h in range(count):
        rest = jnp.where(strict, inverses[h], 0.0).astype(BF16)
        left = stack(known[h].astype(BF16), across[h].astype(BF16))
        out = mm(left, lane_blocks(rest, low, high))
        known[h] = known[h] + out[:tokens]
        across[h] = (across[h] + out[tokens:]).astype(BF16)
    solved = []
    for h in range(count):
        factor = stack(across[h], jnp.zeros_like(across[h]))
        solved.append((known[h] + mm(known[h].astype(BF16), factor)).astype(BF16))

    lane = iota((d, PAIR), 1)
    sub = iota((d, PAIR), 0)
    none = jnp.zeros((d, PAIR), BF16)
    for p, cut in enumerate(cuts):
        away_end = (away[:, cut] * to_end[:, cut]).astype(BF16)
        away_end = side(away_end, jnp.zeros_like(away_end))
        keys_end = side(*split(keys[:, cut] * to_end[:, cut]))
        lefts = [
            side(solved[2 * p + i], stack(none, values[2 * p + i]))
            for i in range(2)
        ]
        ended = folded(stack(*lefts), stack(away_end, keys_end))
        for i in range(2):
            solved_ref[2 * p + i] = lefts[i]
            stay = jnp.where(lane == sub + i * d, gamma_end[:, cut], 0.0)
            state_map = ended[2 * i * d : (2 * i + 1) * d] + stay
            state_add = ended[(2 * i + 1) * d : (2 * i + 2) * d]
            if i == 0:
                state_add = pltpu.roll(state_add, d, 1)
            else:
                state_map = pltpu.roll(state_map, d, 1)
            head = 2 * p + i
            slot = lax.rem(head // per_owner - me % owners + owners, owners)
            held[slot, head % per_owner] = jnp.where(
                lane < d, state_map, state_add
            )

    copies = [
        pltpu.make_async_copy(held.at[k], send_refs[k], sems.at[k])
        for k in range(owners)
    ]
    for copy in copies:
        copy.start()
    for copy in copies:
        copy.wait()


def resident(count):
    return [pl.BlockSpec(memory_space=pltpu.VMEM)] * count


def limit(mib):
    return pltpu.CompilerParams(vmem_limit_bytes=mib << 20)


def range_pass(owners, fade, key, value, removal, rate):
    tokens, features = fade.shape
    heads = features // GROUP_DIMENSION
    block = (heads // owners, GROUP_DIMENSION, PAIR)
    out = pl.pallas_call(
        functools.partial(range_kernel, owners),
        in_specs=[pl.BlockSpec(memory_space=pltpu.HBM)] * 5,
        out_specs=[pl.BlockSpec(memory_space=pl.ANY)] * owners + resident(2),
        out_shape=[jax.ShapeDtypeStruct(block, F32)] * owners
        + [
            jax.ShapeDtypeStruct((heads, tokens, 2 * tokens), BF16),
            jax.ShapeDtypeStruct((5, tokens, features), BF16),
        ],
        scratch_shapes=[
            pltpu.VMEM((owners,) + block, F32),
            pltpu.SemaphoreType.DMA((5,)),
            pltpu.SemaphoreType.DMA((owners,)),
        ],
        compiler_params=limit(40),
        name="range_pass",
    )(fade, key, value, removal, rate)
    return out[:owners], out[owners:]


def read_kernel(
    reader_ref,
    extra_ref,
    solved_ref,
    loaded,
    lift_high_ref,
    lift_low_ref,
    within_ref,
    bonus_ref,
):
    fade_ref, removal_ref, rate_ref, key_ref, value_ref = (
        loaded.at[k] for k in range(loaded.shape[0])
    )
    tokens, width = fade_ref.shape
    d = GROUP_DIMENSION
    ones = group_ones()
    late = late_columns(tokens)
    seen = iota((tokens, tokens), 0) <= iota((tokens, tokens), 1)
    _, cum, middle, past, _, away, keys = key_side(
        fade_ref, removal_ref, rate_ref, key_ref, ones
    )
    reader = reader_ref[...].astype(F32)
    value = value_ref[...].astype(F32)
    bonus = group_sums(reader * key_ref[...].astype(F32) * extra_ref[...], ones)
    bonus_ref[...] = bonus * value
    reader_mid = reader * jnp.exp(past)
    reader_abs = reader_mid * jnp.exp(middle)

    for p in range(width // PAIR):
        cut = slice(p * PAIR, (p + 1) * PAIR)
        early, later = scores(
            late,
            split(away[:, cut]),
            split(keys[:, cut]),
            split(reader_mid[:, cut].T),
            3,
        )
        start = reader_abs[:, cut].T
        for i in range(2):
            lanes = slice(i * tokens, (i + 1) * tokens)
            rows = slice(i * d, (i + 1) * d)
            at = slice(p * PAIR + i * d, p * PAIR + (i + 1) * d)

            def read(part):
                whole = stack(early[part, lanes], later[part, lanes])
                return side(*split(jnp.where(seen, whole, 0.0)))

            out = folded(
                solved_ref[2 * p + i], stack(read(slice(0, d)), read(slice(d, 2 * d)))
            )
            within_ref[at] = out[d:]
            lift_high_ref[at], lift_low_ref[at] = split(start[rows] + out[:d])


def read_pass(reader, extra, solved, loaded):
    tokens, features = reader.shape
    return pl.pallas_call(
        read_kernel,
        in_specs=resident(4),
        out_specs=resident(4),
        out_shape=[
            jax.ShapeDtypeStruct((features, tokens), BF16),
            jax.ShapeDtypeStruct((features, tokens), BF16),
            jax.ShapeDtypeStruct((features, tokens), F32),
            jax.ShapeDtypeStruct((tokens, features), F32),
        ],
        compiler_params=limit(40),
        name="read_pass",
    )(reader, extra, solved, loaded)


def chain_kernel(owners, *refs):
    got_refs = refs[:owners]
    state_refs = refs[owners : 2 * owners]
    final_ref, ranges, states = refs[2 * owners :]
    me = lax.axis_index("seq")
    per_owner = got_refs[0].shape[0]
    for k in range(owners):
        ranges[lax.rem(me - k + owners, owners)] = got_refs[k][...]
    d = GROUP_DIMENSION
    lane = iota((d // 2, PAIR), 1)
    none = jnp.zeros((d, 2 * PAIR), BF16)
    current = []
    for q in range(per_owner):
        states[0, q] = jnp.zeros((d // 2, PAIR), F32)
        current.append(ranges[0, q])
    for i in range(1, owners):
        for q in range(per_owner):
            now = current[q]
            states[i, q] = jnp.where(
                lane < d, pltpu.roll(now[: d // 2], d, 1), now[d // 2 :]
            )
            both = ranges[i, q]
            maps = side(*split(pltpu.roll(both, d, 1)))
            out = mm(stack(*split(now)), stack(none, maps))
            current[q] = out[:d, :PAIR] + out[:d, PAIR:] + out[d:, :PAIR] + both
    for q in range(per_owner):
        final_ref[q * d : (q + 1) * d, :] = pltpu.roll(current[q], d, 1)[:, :d]
    for k in range(owners):
        state_refs[k][...] = states[lax.rem(me + k, owners)]


def chain(got):
    owners = len(got)
    per_owner = got[0].shape[0]
    block = (per_owner, GROUP_DIMENSION // 2, PAIR)
    rows = per_owner * GROUP_DIMENSION
    out = pl.pallas_call(
        functools.partial(chain_kernel, owners),
        in_specs=resident(owners),
        out_specs=resident(owners + 1),
        out_shape=[jax.ShapeDtypeStruct(block, F32)] * owners
        + [jax.ShapeDtypeStruct((rows, GROUP_DIMENSION), F32)],
        scratch_shapes=[
            pltpu.VMEM((owners,) + got[0].shape, F32),
            pltpu.VMEM((owners,) + block, F32),
        ],
        compiler_params=limit(40),
        name="chain",
    )(*got)
    return out[:owners], out[owners]


def finish_kernel(owners, *refs):
    state_refs = refs[:owners]
    lift_high_ref, lift_low_ref, within_ref, bonus_ref, gain_ref = refs[
        owners : owners + 5
    ]
    out_ref, states = refs[owners + 5 :]
    me = lax.axis_index("seq")
    per_owner = state_refs[0].shape[0]
    width = out_ref.shape[1]
    d = GROUP_DIMENSION

    for k in range(owners):
        states[lax.rem(me % owners - k + owners, owners)] = state_refs[k][...]

    lane = iota((d // 2, PAIR), 1)
    results = []
    for head in range(width // d):
        packed = states[head // per_owner, head % per_owner]
        state = split(
            stack(jnp.where(lane < d, packed, 0.0), jnp.where(lane >= d, packed, 0.0))
        )
        at = slice(head * d, (head + 1) * d)
        high, low = lift_high_ref[at], lift_low_ref[at]
        results.append(
            within_ref[at] + mm3(state, (stack(high, high), stack(low, low)))
        )
    for p in range(width // PAIR):
        normed = []
        for result in results[2 * p : 2 * p + 2]:
            average = jnp.mean(result, axis=0, keepdims=True)
            centered = result - average
            spread = jnp.mean(centered * centered, axis=0, keepdims=True)
            normed.append(centered * lax.rsqrt(spread + NORM_EPS))
        cut = slice(p * PAIR, (p + 1) * PAIR)
        turned = stack(*normed).T
        out_ref[:, cut] = (turned * gain_ref[:, cut] + bonus_ref[:, cut]).astype(BF16)


def finish(states, lift_high, lift_low, within, bonus, gain):
    owners = len(states)
    tokens, features = bonus.shape
    return pl.pallas_call(
        functools.partial(finish_kernel, owners),
        in_specs=resident(owners + 5),
        out_specs=resident(1)[0],
        out_shape=jax.ShapeDtypeStruct((tokens, features), BF16),
        scratch_shapes=[pltpu.VMEM((owners,) + states[0].shape, F32)],
        compiler_params=limit(40),
        name="finish",
    )(*states, lift_high, lift_low, within, bonus, gain)


def shifted(value, by, members):
    return lax.ppermute(value, "seq", [(i, (i + by) % members) for i in range(members)])


def relay_states(both, members):
    d = GROUP_DIMENSION
    local_map, local_add = both[:, :, :d], both[:, :, d:]

    def relay(_, carried):
        pairs = [(i, i + 1) for i in range(members - 1)]
        incoming = lax.ppermute(carried[1], "seq", pairs)
        moved = jnp.einsum(
            "hvk,hkj->hvj", incoming, local_map, precision=lax.Precision.HIGHEST
        )
        return (incoming, moved + local_add)

    first = (jnp.zeros_like(local_add), local_add)
    incoming, leaving = lax.fori_loop(0, members - 1, relay, first)
    here = lax.axis_index("seq")
    closing = lax.psum(jnp.where(here == members - 1, leaving, 0.0), "seq")
    closing = closing.reshape(-1, d)
    rows = closing.shape[0] // members
    final = lax.dynamic_slice_in_dim(closing, here * rows, rows, 0)
    packed = jnp.concatenate([incoming[:, : d // 2], incoming[:, d // 2 :]], axis=2)
    return packed, final


def on_device(reader, fade, key, value, removal, rate, extra, gain):
    members = lax.axis_size("seq")
    features = reader.shape[2]
    heads = features // GROUP_DIMENSION
    owners = members if heads % members == 0 else 1
    keyed = (fade[0], key[0], value[0], removal[0], rate[0])
    keyed = [pltpu.with_memory_space_constraint(x, pltpu.HBM) for x in keyed]
    sends, kept = range_pass(owners, *keyed)
    parts = read_pass(reader[0], extra.reshape(1, features), *kept)
    if owners > 1:
        got = [sends[0]] + [shifted(sends[k], k, members) for k in range(1, owners)]
        got, parts = lax.optimization_barrier((got, parts))
        states, final = chain(got)
        states = [states[0]] + [
            shifted(states[k], k, members) for k in range(1, owners)
        ]
    else:
        packed, final = relay_states(sends[0], members)
        states = [packed]
    blended = finish(states, *parts, gain.reshape(1, features))
    return (blended[None], final[None])


def solution(mesh):
    tokens = P(("groups", "dp"), "seq", None)
    return jax.shard_map(
        on_device,
        mesh=mesh,
        in_specs=(tokens,) * 6 + (P(), P()),
        out_specs=(tokens, tokens),
        check_vma=False,
    )
```
